768 devices in a mesh: space: 192 (over z, y_lo, x), tm: 4 (over y_hi, core).
Axes of the slice: x: 4, y: 8 (y_hi: 2, y_lo: 4; y = y_hi * 4 + y_lo), z: 12, core: 2. Of those that a mesh axis runs over, the one named last changes fastest.
Arguments:
- eigvecs: float32 [4, 2, 3, 64, 192, 144], P('tm', None, None, None, 'space'), may hold values from -6 to 6
- gauge_links: float32 [3, 4, 2, 3, 3, 192, 144], P(None, 'tm', None, None, None, 'space'), may hold values from -4 to 4
- perambulators: bfloat16 [4, 4, 2, 4, 4, 64, 64], P('tm'), may hold values from -0.375 to 0.375
- momenta: int32 [32, 3], replicated, may hold values from -2 to 2, as said below
Outputs:
- smeared: bfloat16 [4, 2, 3, 64, 192, 144], P('tm', None, None, None, 'space')
- elementals: bfloat16 [32, 4, 2, 64, 64], P(None, 'tm')
- correlator: float32 [2, 32, 4, 4], P(None, None, 'tm')
The draws below stay inside these ranges and needn't reach their ends.
Inputs may be any that keep to these rules, and one draw needn't show every extreme that they name: `momenta`: every row is a nonzero vector of integers.
All inputs are finite; a program needn't handle non-finite values.
Results may differ from the reference program's by a relative error of at most 0.0053.
Values may be sent and summed in bfloat16 or wider, within the bound.
No kernel may reach another device: no remote copies, remote signals or barrier semaphores. Data moves between devices by JAX's collectives and lax.ppermute only.
A program may use at most 32 MiB of HBM per device.

```python
import math
import jax
import jax.numpy as jnp
from jax import lax

NEV = 64
NP = 32
SPIN = 4
LX = 24
YB = 4
NT = 4
NZ = 48
ROWS = 6


def draw_momenta(key, part):
    sampled = jax.random.randint(key, (NP, 3), -2, 3, dtype=jnp.int32)
    zero_row = jnp.all(sampled == 0, axis=1)
    first_col = jnp.where(zero_row, 1, sampled[:, 0])
    sampled = jnp.concatenate([first_col[:, None], sampled[:, 1:]], axis=1)
    forced = jnp.array([[2, -2, 1]], dtype=jnp.int32)
    row_ids = jnp.arange(NP, dtype=jnp.int32)[:, None]
    return jnp.where(row_ids == 0, forced, sampled).astype(jnp.int32)


def block_scale(key, dims, split, smallest, top_value):
    factor_of = 1.0
    for position, shards_of in split:
        steps = jax.random.uniform(jax.random.fold_in(jax.random.fold_in(key, 6), position), (shards_of,), jnp.float32, smallest / len(split), top_value / len(split))
        factor_of = factor_of * jnp.repeat(jnp.exp(steps), dims[position] // shards_of).reshape((-1,) + (1,) * (len(dims) - 1 - position))
    return factor_of


def centred(own_key, extent, spread, limit, pieces=(), kind=jnp.bfloat16):
    factor_of = block_scale(own_key, extent, pieces, -0.22, 0.18) if pieces else 1.0
    values = jax.random.normal(own_key, extent, jnp.float32) * spread * factor_of
    return jnp.minimum(jnp.maximum(values, -limit), limit).astype(kind)


def setup_inputs(seed: int = 0) -> dict:
    key_of = jax.random.split(jax.random.key(seed), 5)
    eigvecs = centred(key_of[0], (NT, 2, 3, NEV, NZ * YB, ROWS * LX), 1.0, 6.0, ((0, 4), (4, 192)), jnp.float32)
    gauge_links = centred(key_of[1], (3, NT, 2, 3, 3, NZ * YB, ROWS * LX), 0.577, 4.0, ((1, 4), (5, 192)), jnp.float32)
    perambulators = centred(key_of[2], (NT, NT, 2, SPIN, SPIN, NEV, NEV), (NEV * SPIN) ** -0.5, 0.375, ((0, 4),))
    momenta = draw_momenta(jax.random.fold_in(key_of[4], 71), 0)
    return {"eigvecs": eigvecs, "gauge_links": gauge_links, "perambulators": perambulators, "momenta": momenta}


KAPPA = 0.25
op_group = 2

def move(lattice, direction, stride):
    layout = lattice.shape
    planes = lattice.reshape(layout[:-1] + (layout[-1] // LX, LX))
    if direction == 0:
        planes = jnp.roll(planes, -stride, axis=-1)
    elif direction == 1:
        planes = jnp.roll(planes, -stride, axis=-2)
    else:
        planes = jnp.roll(planes, -stride, axis=-3)
    return planes.reshape(layout)

def transport(one_link, vector, adjoint):
    link_re = one_link[..., 0, :, :, :, :]
    link_im = one_link[..., 1, :, :, :, :]
    vec_re = vector[..., 0, :, :, :, :]
    vec_im = vector[..., 1, :, :, :, :]
    out_re = 0.0
    out_im = 0.0
    for colour in range(3):
        if adjoint:
            factor_re = link_re[..., colour, :, None, :, :]
            factor_im = -link_im[..., colour, :, None, :, :]
        else:
            factor_re = link_re[..., :, colour, None, :, :]
            factor_im = link_im[..., :, colour, None, :, :]
        source_re = vec_re[..., colour:colour + 1, :, :, :]
        source_im = vec_im[..., colour:colour + 1, :, :, :]
        out_re = out_re + factor_re * source_re - factor_im * source_im
        out_im = out_im + factor_re * source_im + factor_im * source_re
    return jnp.stack([out_re, out_im], axis=-5)

def smear(vector, gauge):
    summed = (1.0 - 6.0 * KAPPA) * vector
    for direction in range(3):
        one_link = gauge[direction]
        forward = transport(one_link, move(vector, direction, 1), False)
        behind = move(transport(one_link, vector, True), direction, -1)
        summed = summed + KAPPA * (forward + behind)
    return summed

def phases(momenta, z_start, z_count, z_total):
    site_index = jnp.arange(LX * LX, dtype=jnp.int32)
    x_coord = site_index % LX
    y_coord = site_index // LX
    z_coord = z_start + jnp.arange(z_count, dtype=jnp.int32)
    turn_x = momenta[:, 0, None] * x_coord[None] % LX
    turn_y = momenta[:, 1, None] * y_coord[None] % LX
    turn_z = momenta[:, 2, None] * z_coord[None] % z_total
    angles = 2.0 * math.pi * (turn_x.astype(jnp.float32)[:, None, :] / LX + turn_y.astype(jnp.float32)[:, None, :] / LX + turn_z.astype(jnp.float32)[:, :, None] / z_total)
    return (jnp.cos(angles), -jnp.sin(angles))

def contract(smeared, cos_part, sin_part, norm_scale):
    smear_re = smeared[:, 0].astype(jnp.float32)
    smear_im = smeared[:, 1].astype(jnp.float32)
    cos_wide = cos_part[:, None, None, None]
    sin_wide = sin_part[:, None, None, None]
    phased_re = (smear_re[None] * cos_wide - smear_im[None] * sin_wide).astype(jnp.bfloat16)
    phased_im = (smear_re[None] * sin_wide + smear_im[None] * cos_wide).astype(jnp.bfloat16)
    phased = jnp.stack([phased_re, phased_im], axis=2)
    product = jnp.einsum('tlcazs,ptmcbzs->ptlamb', smeared.astype(jnp.float32), phased.astype(jnp.float32), precision=lax.Precision.HIGHEST)
    elem_re = product[:, :, 0, :, 0] + product[:, :, 1, :, 1]
    elem_im = product[:, :, 0, :, 1] - product[:, :, 1, :, 0]
    return norm_scale * jnp.stack([elem_re, elem_im], axis=2)

def reference(eigvecs, gauge_links, perambulators, momenta):
    norm_scale = 1.0 / math.sqrt(3.0 * NZ * LX * LX)
    cos_all, sin_all = phases(momenta, 0, NZ, NZ)

    def per_slice(slice_pair):
        vector, gauge = slice_pair
        vector = vector.reshape(vector.shape[:-2] + (NZ, LX * LX))
        gauge = gauge.reshape(gauge.shape[:-2] + (NZ, LX * LX))
        smeared_nat = smear(vector, gauge).astype(jnp.bfloat16)
        smeared = smeared_nat[None]

        def per_group(group_index):
            cos_group = lax.dynamic_slice_in_dim(cos_all, group_index * op_group, op_group, 0)
            sin_group = lax.dynamic_slice_in_dim(sin_all, group_index * op_group, op_group, 0)
            return contract(smeared, cos_group, sin_group, norm_scale)[:, 0]
        grouped = lax.map(per_group, jnp.arange(NP // op_group, dtype=jnp.int32))
        blocked = smeared_nat.reshape(smeared_nat.shape[:-2] + (NZ * YB, ROWS * LX))
        return (grouped.reshape((NP, 2, NEV, NEV)), blocked)
    raw, smeared_out = lax.map(per_slice, (eigvecs, jnp.moveaxis(gauge_links, 1, 0)))
    elementals = jnp.moveaxis(raw, 0, 1).astype(jnp.bfloat16)
    phi_bf = elementals
    blocks = perambulators.reshape((NT, NT, 2, SPIN * SPIN, NEV, NEV)).astype(jnp.float32)
    tau_re = blocks[:, :, 0]
    tau_im = blocks[:, :, 1]
    high = lax.Precision.HIGHEST

    def per_op(phi_op):
        remote = phi_op.astype(jnp.float32)
        far_re = remote[:, 0]
        far_im = remote[:, 1]
        left_re = jnp.einsum('tnqia,nba->tnqib', tau_re, far_re, precision=high) + jnp.einsum('tnqia,nba->tnqib', tau_im, far_im, precision=high)
        left_im = jnp.einsum('tnqia,nba->tnqib', tau_im, far_re, precision=high) - jnp.einsum('tnqia,nba->tnqib', tau_re, far_im, precision=high)
        left_re = lax.optimization_barrier(left_re.astype(jnp.bfloat16)).astype(jnp.float32)
        left_im = lax.optimization_barrier(left_im.astype(jnp.bfloat16)).astype(jnp.float32)
        right_re = jnp.einsum('tnqib,tnqkb->tnqik', left_re, tau_re, precision=high) + jnp.einsum('tnqib,tnqkb->tnqik', left_im, tau_im, precision=high)
        right_im = jnp.einsum('tnqib,tnqkb->tnqik', left_im, tau_re, precision=high) - jnp.einsum('tnqib,tnqkb->tnqik', left_re, tau_im, precision=high)
        corr_re = jnp.einsum('tab,tnqba->tn', far_re, right_re, precision=high) - jnp.einsum('tab,tnqba->tn', far_im, right_im, precision=high)
        corr_im = jnp.einsum('tab,tnqba->tn', far_re, right_im, precision=high) + jnp.einsum('tab,tnqba->tn', far_im, right_re, precision=high)
        return jnp.stack([corr_re, corr_im]) / NEV
    correlator = lax.map(per_op, phi_bf)
    return (smeared_out, elementals, jnp.moveaxis(correlator, 1, 0))
```

```python
import math

import jax
import jax.numpy as jnp
from jax import lax
from jax.experimental import pallas as pl
from jax.experimental.pallas import tpu as pltpu
from jax.sharding import Mesh, PartitionSpec as P

NEV = 64
LX = 24
NZ = 48
SITES = 144
ROW = LX
KAPPA = 0.25
F32 = jnp.float32
BF16 = jnp.bfloat16
NT_DIMS = (((1,), (1,)), ((), ()))

USE_PALLAS = True


def roll(x, shift, axis):
    shift = shift % x.shape[axis]
    if USE_PALLAS:
        return pltpu.roll(x, shift, axis)
    return jnp.roll(x, shift, axis)


def half_sign(shape, low):
    lane = lax.broadcasted_iota(jnp.int32, shape, len(shape) - 1)
    return jnp.where(lane < 64, low, -low).astype(F32)


def turned(x):
    return roll(x, 64, 1) * half_sign(x.shape, -1.0)


def link(cols, mu, part, row, col, lo, hi):
    index = ((mu * 2 + part) * 3 + row) * 3 + col
    return cols[lo:hi, index : index + 1]


def carry(cols, mu, values, adjoint, lo, hi):
    spun = [turned(v) for v in values]
    out = []
    for i in range(3):
        total = None
        for j in range(3):
            if adjoint:
                term = link(cols, mu, 0, j, i, lo, hi) * values[j] - link(cols, mu, 1, j, i, lo, hi) * spun[j]
            else:
                term = link(cols, mu, 0, i, j, lo, hi) * values[j] + link(cols, mu, 1, i, j, lo, hi) * spun[j]
            total = term if total is None else total + term
        out.append(total)
    return out


def kernel_prepare(v_ref, g_ref, vt_ref, bz_ref, yf_ref, yb_ref, cols_ref):
    cols = g_ref[...].T
    cols_ref[...] = cols
    values = []
    for c in range(3):
        both = jnp.concatenate([v_ref[0, c], v_ref[1, c]], axis=0)
        values.append(both.T)
    for c in range(3):
        vt_ref[c] = values[c]
        yf_ref[c] = values[c][:ROW]
    back = carry(cols, 2, values, True, 0, SITES)
    edge = carry(cols, 1, [v[SITES - ROW :] for v in values], True, SITES - ROW, SITES)
    for c in range(3):
        bz_ref[c] = back[c]
        yb_ref[c] = edge[c]


def kernel_inner(vt_ref, cols_ref, acc_ref):
    cols = cols_ref[...]
    values = [vt_ref[c] for c in range(3)]
    x_coord = lax.broadcasted_iota(jnp.int32, (SITES, 128), 0) % LX
    ahead = [jnp.where(x_coord == LX - 1, roll(v, LX - 1, 0), roll(v, -1, 0)) for v in values]
    fwd = carry(cols, 0, ahead, False, 0, SITES)
    back = carry(cols, 0, values, True, 0, SITES)
    back = [jnp.where(x_coord == 0, roll(b, -(LX - 1), 0), roll(b, 1, 0)) for b in back]
    up = carry(cols, 1, [v[ROW:] for v in values], False, 0, SITES - ROW)
    down = carry(cols, 1, [v[: SITES - ROW] for v in values], True, 0, SITES - ROW)
    zero = jnp.zeros((ROW, 128), F32)
    for c in range(3):
        inner_y = jnp.concatenate([up[c], zero], axis=0) + jnp.concatenate([zero, down[c]], axis=0)
        acc_ref[c] = (1.0 - 6.0 * KAPPA) * values[c] + KAPPA * (fwd[c] + back[c]) + KAPPA * inner_y


def kernel_smear(acc_ref, cols_ref, above_ref, bz_ref, ya_ref, yb_ref, send_ref, out_ref):
    cols = cols_ref[...]
    fwd = carry(cols, 2, [above_ref[c] for c in range(3)], False, 0, SITES)
    edge = carry(cols, 1, [ya_ref[c] for c in range(3)], False, SITES - ROW, SITES)
    middle = jnp.zeros((SITES - 2 * ROW, 128), F32)
    for c in range(3):
        rims = jnp.concatenate([yb_ref[c], middle, edge[c]], axis=0)
        total = acc_ref[c] + KAPPA * rims + KAPPA * (fwd[c] + bz_ref[c])
        rounded = total.astype(BF16)
        for k in range(4):
            send_ref[k, c] = rounded
        flat = rounded.astype(F32).T
        out_ref[0, c] = flat[:64].astype(BF16)
        out_ref[1, c] = flat[64:].astype(BF16)


def kernel_contract(s_ref, ph_ref, out_ref, wide_ref, spun_ref, *, scale):
    rows = 4 * 3 * SITES
    lhs = []
    for k in range(4):
        for c in range(3):
            at = (k * 3 + c) * SITES
            wide = s_ref[k, c].astype(F32)
            wide_ref[at : at + SITES] = wide
            spun_ref[at : at + SITES] = turned(wide)
            lhs.append(wide.T.astype(BF16))
    lhs = jnp.concatenate(lhs, axis=1)
    phase = ph_ref[...].T
    sign = half_sign((64, 128), 1.0)
    for yl in range(4):
        pair = []
        for pp in range(2):
            p = yl * 2 + pp
            parts = []
            for k in range(4):
                cos = jnp.broadcast_to(phase[k * SITES : (k + 1) * SITES, p : p + 1], (SITES, 128))
                sin = jnp.broadcast_to(phase[k * SITES : (k + 1) * SITES, 8 + p : 9 + p], (SITES, 128))
                for c in range(3):
                    at = (k * 3 + c) * SITES
                    parts.append((wide_ref[at : at + SITES] * cos + spun_ref[at : at + SITES] * sin).astype(BF16))
            pair.append(jnp.concatenate(parts, axis=0))
        both = jnp.concatenate(pair, axis=1)
        prod = jnp.dot(lhs, both, preferred_element_type=F32)
        for pp in range(2):
            block = prod[:, pp * 128 : (pp + 1) * 128]
            result = (block[:64] + roll(block[64:], 64, 1) * sign) * scale
            out_ref[pp * 2, yl] = result[:32]
            out_ref[pp * 2 + 1, yl] = result[32:]


def kernel_correlate(tm_ref, e_ref, b1_ref, b2_ref, out_ref):
    own = tm_ref[0]
    flip = []
    for pp in range(2):
        phi = jnp.concatenate([e_ref[2 * pp, own], e_ref[2 * pp + 1, own]], axis=0)
        for k in range(16):
            out_ref[k, pp * 64 : (pp + 1) * 64] = phi
        tall = phi.astype(F32).T
        flip.append(jnp.concatenate([tall[:64], tall[64:]], axis=1))
    sign = half_sign((64, 128), 1.0)
    row = lax.broadcasted_iota(jnp.int32, (16, 128), 0)
    lane = lax.broadcasted_iota(jnp.int32, (16, 128), 1)
    tile = jnp.zeros((16, 128), F32)
    for t0 in range(4):
        weights = []
        for pp in range(2):
            far = jnp.concatenate([e_ref[2 * pp, t0], e_ref[2 * pp + 1, t0]], axis=0)
            weights.append(far)
            weights.append(turned(far.astype(F32)).astype(BF16))
        weights = jnp.concatenate(weights, axis=0)
        left = lax.dot_general(b1_ref[t0], weights, NT_DIMS, preferred_element_type=F32).astype(BF16)
        tall = []
        for pp in range(2):
            tall.append(
                jnp.concatenate([left[q * 64 : (q + 1) * 64, pp * 128 : (pp + 1) * 128] for q in range(16)], axis=1)
            )
        tall = jnp.concatenate(tall, axis=0)
        right = lax.dot_general(tall, b2_ref[t0], NT_DIMS, preferred_element_type=F32)
        for pp in range(2):
            block = right[pp * 64 : (pp + 1) * 64]
            real = jnp.sum(flip[pp] * block * sign) * (1.0 / NEV)
            imag = jnp.sum(flip[pp] * roll(block, 64, 1)) * (1.0 / NEV)
            here = row == pp * 4 + t0
            tile = jnp.where(here & (lane % 2 == 0), real, tile)
            tile = jnp.where(here & (lane % 2 == 1), imag, tile)
    high = tile.astype(BF16).astype(F32)
    middle = (tile - high).astype(BF16).astype(F32)
    low = tile - high - middle
    packed = jnp.where(lane < 2, high, jnp.where(lane < 4, middle, low)).astype(BF16)
    for k in range(16):
        out_ref[k, 128:144] = packed


def kernel_unpack(r_ref, e_ref):
    for s in range(16):
        for pp in range(2):
            both = r_ref[s, pp * 64 : (pp + 1) * 64]
            e_ref[2 * s + pp, 0] = both[:, :64]
            e_ref[2 * s + pp, 1] = both[:, 64:]


def shape(dims, dtype):
    return jax.ShapeDtypeStruct(dims, dtype)


def run(kernel, outs, args, name, scratch=(), scalar=False):
    in_specs = None
    if scalar:
        in_specs = [pl.BlockSpec(memory_space=pltpu.SMEM)] + [pl.BlockSpec(memory_space=pltpu.VMEM)] * (len(args) - 1)
    else:
        in_specs = [pl.BlockSpec(memory_space=pltpu.VMEM)] * len(args)
    return pl.pallas_call(
        kernel,
        out_shape=outs,
        in_specs=in_specs,
        out_specs=jax.tree.map(lambda _: pl.BlockSpec(memory_space=pltpu.VMEM), outs),
        scratch_shapes=list(scratch),
        name=name,
        compiler_params=pltpu.CompilerParams(vmem_limit_bytes=48 << 20),
    )(*args)


def phases(momenta, z_index):
    site = jnp.arange(4 * SITES, dtype=jnp.int32)
    turn_x = momenta[:, 0, None] * (site % LX)[None] % LX
    turn_y = momenta[:, 1, None] * (site // LX)[None] % LX
    turn_z = momenta[:, 2, None] * z_index % NZ
    angles = (
        2.0
        * math.pi
        * (turn_x.astype(F32) / LX + turn_y.astype(F32) / LX + turn_z.astype(F32) / NZ)
    )
    return jnp.concatenate([jnp.cos(angles), -jnp.sin(angles)], axis=0)


def swap(value, axes):
    return lax.all_to_all(value, axes, split_axis=0, concat_axis=0, tiled=True)


def spread(value, axes, count):
    return swap(jnp.broadcast_to(value[None], (count,) + value.shape), axes)


def local(eigvecs, gauge_links, perambulators, momenta):
    planes = ("zh", "zl", "yl")
    up = [(i, (i + 1) % NZ) for i in range(NZ)]
    down = [((i + 1) % NZ, i) for i in range(NZ)]
    ring_up = [(i, (i + 1) % 4) for i in range(4)]
    ring_down = [((i + 1) % 4, i) for i in range(4)]
    z_index = lax.axis_index(planes)
    x_index = lax.axis_index("x")
    tm_index = lax.axis_index(("yh", "c"))

    field = eigvecs.reshape(2, 3, NEV, SITES)
    links = gauge_links.reshape(54, SITES)
    site_shape = shape((3, SITES, 128), F32)
    row_shape = shape((3, ROW, 128), F32)
    values, back_z, first_row, last_row, cols = run(
        kernel_prepare,
        (site_shape, site_shape, row_shape, row_shape, shape((SITES, 54), F32)),
        (field, links),
        "prepare",
    )
    above = lax.ppermute(values, planes, down)
    below = lax.ppermute(back_z, planes, up)
    row_above = lax.ppermute(first_row, "x", ring_down)
    row_below = lax.ppermute(last_row, "x", ring_up)

    inner = run(kernel_inner, site_shape, (values, cols), "inner")
    mine = lax.dynamic_index_in_dim(momenta.reshape(4, 4, 2, 3), x_index, 1, keepdims=False).reshape(8, 3)
    phase = phases(mine, z_index)
    blocks = perambulators.reshape(4, 2, 16, NEV, NEV)
    tau_re = blocks[:, 0]
    tau_im = blocks[:, 1]
    straight = jnp.concatenate([tau_re, tau_im], axis=-1)
    crossed = jnp.concatenate([-tau_im, tau_re], axis=-1)
    first_factor = straight.reshape(4, 16 * NEV, 128)
    second_factor = jnp.concatenate(
        [
            jnp.swapaxes(straight, 1, 2).reshape(4, NEV, 16 * 128),
            jnp.swapaxes(crossed, 1, 2).reshape(4, NEV, 16 * 128),
        ],
        axis=1,
    )

    send, smeared = run(
        kernel_smear,
        (shape((4, 3, SITES, 128), BF16), shape((2, 3, NEV, SITES), BF16)),
        (inner, cols, above, below, row_above, row_below),
        "smear",
    )
    shared = swap(send, "x")
    scale = 1.0 / math.sqrt(3.0 * NZ * LX * LX)

    def contract(*refs):
        kernel_contract(*refs, scale=scale)

    partial = run(
        contract,
        shape((4, 4, 32, 128), F32),
        (shared, phase),
        "contract",
        scratch=[pltpu.VMEM((12 * SITES, 128), F32), pltpu.VMEM((12 * SITES, 128), F32)],
    )
    pieces = swap(partial.reshape(16, 32, 128), ("zl", "yl"))
    part = jnp.sum(pieces, axis=0)
    part = jnp.sum(spread(part, "zh", 3), axis=0)
    near = spread(part.astype(BF16), ("zl", "yh", "c"), 16).reshape(4, 4, 32, 128)
    payload = run(
        kernel_correlate,
        shape((16, 144, 128), BF16),
        (tm_index.astype(jnp.int32).reshape(1), near, first_factor, second_factor),
        "correlate",
        scalar=True,
    )
    everything = swap(payload, ("yl", "x"))
    elementals = run(kernel_unpack, shape((32, 2, NEV, NEV), BF16), (everything,), "unpack")
    terms = everything[:, 128:136, :6].astype(F32).reshape(16, 2, 4, 3, 2)
    correlator = (terms[..., 0, :] + terms[..., 1, :]) + terms[..., 2, :]
    correlator = jnp.moveaxis(correlator.reshape(32, 4, 2), 2, 0)
    return (
        smeared.reshape(1, 2, 3, NEV, 1, SITES),
        elementals.reshape(32, 1, 2, NEV, NEV),
        correlator.reshape(2, 32, 1, 4),
    )


def solution(mesh):
    fine = Mesh(mesh.devices.reshape(3, 4, 4, 4, 2, 2), ("zh", "zl", "yl", "x", "yh", "c"))
    space = ("zh", "zl", "yl", "x")
    times = ("yh", "c")
    return jax.shard_map(
        local,
        mesh=fine,
        in_specs=(
            P(times, None, None, None, space, None),
            P(None, times, None, None, None, space, None),
            P(times, None, None, None, None, None, None),
            P(),
        ),
        out_specs=(
            P(times, None, None, None, space, None),
            P(None, times, None, None, None),
            P(None, None, times, None),
        ),
        check_vma=False,
    )
```

```python
import math

import jax
import jax.numpy as jnp
from jax import lax
from jax.experimental import pallas as pl
from jax.experimental.pallas import tpu as pltpu
from jax.sharding import Mesh, PartitionSpec as P


NEV = 64
LX = 24
NZ = 48
SITES = 144
ROW = LX
KAPPA = 0.25
F32 = jnp.float32
BF16 = jnp.bfloat16
NT_DIMS = (((1,), (1,)), ((), ()))

USE_PALLAS = True


def roll(x, shift, axis):
    shift = shift % x.shape[axis]
    if USE_PALLAS:
        return pltpu.roll(x, shift, axis)
    return jnp.roll(x, shift, axis)


def half_sign(shape, low):
    lane = lax.broadcasted_iota(jnp.int32, shape, len(shape) - 1)
    return jnp.where(lane < 64, low, -low).astype(F32)


def turned(x):
    return roll(x, 64, 1) * half_sign(x.shape, -1.0)


def link(cols, mu, part, row, col, lo, hi):
    index = ((mu * 2 + part) * 3 + row) * 3 + col
    return cols[lo:hi, index : index + 1]


def carry(cols, mu, values, adjoint, lo, hi):
    spun = [turned(v) for v in values]
    out = []
    for i in range(3):
        total = None
        for j in range(3):
            if adjoint:
                term = link(cols, mu, 0, j, i, lo, hi) * values[j] - link(cols, mu, 1, j, i, lo, hi) * spun[j]
            else:
                term = link(cols, mu, 0, i, j, lo, hi) * values[j] + link(cols, mu, 1, i, j, lo, hi) * spun[j]
            total = term if total is None else total + term
        out.append(total)
    return out


def kernel_prepare(odd_ref, v_ref, g_ref, vt_ref, za_ref, zb_ref, xa_ref, xb_ref, cols_ref):
    cols = g_ref[:, 0, :].T
    cols_ref[...] = cols
    values = []
    for c in range(3):
        both = jnp.concatenate([v_ref[c * 64 : (c + 1) * 64, 0, :], v_ref[192 + c * 64 : 256 + c * 64, 0, :]], axis=0)
        values.append(both.T)
    back = carry(cols, 2, values, True, 0, SITES)
    edge = carry(cols, 1, [v[SITES - ROW :] for v in values], True, SITES - ROW, SITES)
    plane_odd = odd_ref[0] == 1
    block_odd = odd_ref[1] == 1
    for c in range(3):
        vt_ref[c] = values[c]
        za_ref[c] = jnp.where(plane_odd, values[c], back[c])
        zb_ref[c] = jnp.where(plane_odd, back[c], values[c])
        xa_ref[c] = jnp.where(block_odd, values[c][:ROW], edge[c])
        xb_ref[c] = jnp.where(block_odd, edge[c], values[c][:ROW])


def kernel_inner(vt_ref, cols_ref, acc_ref):
    cols = cols_ref[...]
    values = [vt_ref[c] for c in range(3)]
    x_coord = lax.broadcasted_iota(jnp.int32, (SITES, 128), 0) % LX
    ahead = [jnp.where(x_coord == LX - 1, roll(v, LX - 1, 0), roll(v, -1, 0)) for v in values]
    fwd = carry(cols, 0, ahead, False, 0, SITES)
    back = carry(cols, 0, values, True, 0, SITES)
    back = [jnp.where(x_coord == 0, roll(b, -(LX - 1), 0), roll(b, 1, 0)) for b in back]
    up = carry(cols, 1, [v[ROW:] for v in values], False, 0, SITES - ROW)
    down = carry(cols, 1, [v[: SITES - ROW] for v in values], True, 0, SITES - ROW)
    zero = jnp.zeros((ROW, 128), F32)
    for c in range(3):
        inner_y = jnp.concatenate([up[c], zero], axis=0) + jnp.concatenate([zero, down[c]], axis=0)
        acc_ref[c] = (1.0 - 6.0 * KAPPA) * values[c] + KAPPA * (fwd[c] + back[c]) + KAPPA * inner_y


def kernel_smear(odd_ref, acc_ref, cols_ref, za_ref, zb_ref, xa_ref, xb_ref, send_ref, out_ref):
    cols = cols_ref[...]
    plane_odd = odd_ref[0] == 1
    block_odd = odd_ref[1] == 1
    fwd = carry(cols, 2, [jnp.where(plane_odd, zb_ref[c], za_ref[c]) for c in range(3)], False, 0, SITES)
    edge = carry(cols, 1, [jnp.where(block_odd, xb_ref[c], xa_ref[c]) for c in range(3)], False, SITES - ROW, SITES)
    middle = jnp.zeros((SITES - 2 * ROW, 128), F32)
    for c in range(3):
        below = jnp.where(plane_odd, za_ref[c], zb_ref[c])
        row_below = jnp.where(block_odd, xa_ref[c], xb_ref[c])
        rims = jnp.concatenate([row_below, middle, edge[c]], axis=0)
        total = acc_ref[c] + KAPPA * rims + KAPPA * (fwd[c] + below)
        rounded = total.astype(BF16)
        for k in range(4):
            send_ref[k, c] = rounded
        flat = rounded.astype(F32).T
        out_ref[0, c] = flat[:64].astype(BF16)
        out_ref[1, c] = flat[64:].astype(BF16)


def kernel_contract(s_ref, ph_ref, out_ref, wide_ref, spun_ref, *, scale):
    lhs = []
    for k in range(4):
        for c in range(3):
            at = (k * 3 + c) * SITES
            wide = s_ref[k, c].astype(F32)
            wide_ref[at : at + SITES] = wide
            spun_ref[at : at + SITES] = turned(wide)
            lhs.append(wide.T.astype(BF16))
    lhs = jnp.concatenate(lhs, axis=1)
    phase = ph_ref[...].T
    sign = half_sign((64, 128), 1.0)
    for yl in range(4):
        pair = []
        for pp in range(2):
            p = yl * 2 + pp
            parts = []
            for k in range(4):
                cos = jnp.broadcast_to(phase[k * SITES : (k + 1) * SITES, p : p + 1], (SITES, 128))
                sin = jnp.broadcast_to(phase[k * SITES : (k + 1) * SITES, 8 + p : 9 + p], (SITES, 128))
                for c in range(3):
                    at = (k * 3 + c) * SITES
                    parts.append((wide_ref[at : at + SITES] * cos + spun_ref[at : at + SITES] * sin).astype(BF16))
            pair.append(jnp.concatenate(parts, axis=0))
        both = jnp.concatenate(pair, axis=1)
        prod = jnp.dot(lhs, both, preferred_element_type=F32)
        for pp in range(2):
            block = prod[:, pp * 128 : (pp + 1) * 128]
            result = (block[:64] + roll(block[64:], 64, 1) * sign) * scale
            out_ref[pp * 2, yl] = result[:32]
            out_ref[pp * 2 + 1, yl] = result[32:]


def kernel_factors(p_ref, out_ref):
    for t0 in range(4):
        for q in range(16):
            real = p_ref[t0, 0, q].astype(F32)
            imag = p_ref[t0, 1, q].astype(F32)
            at = q * 128
            out_ref[t0, :64, at : at + 128] = jnp.concatenate([real, imag], axis=1).astype(BF16)
            out_ref[t0, 64:, at : at + 128] = jnp.concatenate([-imag, real], axis=1).astype(BF16)


def kernel_correlate(tm_ref, e_ref, b_ref, out_ref):
    own = tm_ref[0]
    flip = []
    for pp in range(2):
        phi = jnp.concatenate([e_ref[2 * pp, own], e_ref[2 * pp + 1, own]], axis=0)
        for k in range(16):
            out_ref[k, pp * 64 : (pp + 1) * 64] = phi
        tall = phi.astype(F32).T
        flip.append(jnp.concatenate([tall[:64], tall[64:]], axis=1))
    sign = half_sign((64, 128), 1.0)
    row = lax.broadcasted_iota(jnp.int32, (16, 128), 0)
    lane = lax.broadcasted_iota(jnp.int32, (16, 128), 1)
    tile = jnp.zeros((16, 128), F32)
    for t0 in range(4):
        weights = []
        for pp in range(2):
            far = jnp.concatenate([e_ref[2 * pp, t0], e_ref[2 * pp + 1, t0]], axis=0)
            weights.append(far)
            weights.append(turned(far.astype(F32)).astype(BF16))
        weights = jnp.concatenate(weights, axis=0)
        first = jnp.concatenate([b_ref[t0, :64, q * 128 : (q + 1) * 128] for q in range(16)], axis=0)
        left = lax.dot_general(first, weights, NT_DIMS, preferred_element_type=F32).astype(BF16)
        tall = []
        for pp in range(2):
            tall.append(
                jnp.concatenate([left[q * 64 : (q + 1) * 64, pp * 128 : (pp + 1) * 128] for q in range(16)], axis=1)
            )
        tall = jnp.concatenate(tall, axis=0)
        right = lax.dot_general(tall, b_ref[t0], NT_DIMS, preferred_element_type=F32)
        for pp in range(2):
            block = right[pp * 64 : (pp + 1) * 64]
            real = jnp.sum(flip[pp] * block * sign) * (1.0 / NEV)
            imag = jnp.sum(flip[pp] * roll(block, 64, 1)) * (1.0 / NEV)
            here = row == pp * 4 + t0
            tile = jnp.where(here & (lane % 2 == 0), real, tile)
            tile = jnp.where(here & (lane % 2 == 1), imag, tile)
    high = tile.astype(BF16).astype(F32)
    middle = (tile - high).astype(BF16).astype(F32)
    low = tile - high - middle
    packed = jnp.where(lane < 2, high, jnp.where(lane < 4, middle, low)).astype(BF16)
    for k in range(16):
        out_ref[k, 128:144] = packed


def kernel_unpack(r_ref, e_ref):
    for s in range(16):
        for pp in range(2):
            both = r_ref[s, pp * 64 : (pp + 1) * 64]
            e_ref[2 * s + pp, 0] = both[:, :64]
            e_ref[2 * s + pp, 1] = both[:, 64:]


def shape(dims, dtype):
    return jax.ShapeDtypeStruct(dims, dtype)


def run(kernel, outs, args, scratch=(), scalar=False):
    in_specs = None
    if scalar:
        in_specs = [pl.BlockSpec(memory_space=pltpu.SMEM)] + [pl.BlockSpec(memory_space=pltpu.VMEM)] * (len(args) - 1)
    else:
        in_specs = [pl.BlockSpec(memory_space=pltpu.VMEM)] * len(args)
    return pl.pallas_call(
        kernel,
        out_shape=outs,
        in_specs=in_specs,
        out_specs=jax.tree.map(lambda _: pl.BlockSpec(memory_space=pltpu.VMEM), outs),
        scratch_shapes=list(scratch),
        compiler_params=pltpu.CompilerParams(vmem_limit_bytes=48 << 20),
    )(*args)


def phases(momenta, z_index):
    site = jnp.arange(4 * SITES, dtype=jnp.int32)
    turn_x = momenta[:, 0, None] * (site % LX)[None] % LX
    turn_y = momenta[:, 1, None] * (site // LX)[None] % LX
    turn_z = momenta[:, 2, None] * z_index % NZ
    angles = (
        2.0
        * math.pi
        * (turn_x.astype(F32) / LX + turn_y.astype(F32) / LX + turn_z.astype(F32) / NZ)
    )
    return jnp.concatenate([jnp.cos(angles), -jnp.sin(angles)], axis=0)


def swap(value, axes):
    return lax.all_to_all(value, axes, split_axis=0, concat_axis=0, tiled=True)


def spread(value, axes, count):
    return swap(jnp.broadcast_to(value[None], (count,) + value.shape), axes)


def local(eigvecs, gauge_links, perambulators, momenta):
    planes = ("zh", "zl", "yl")
    pairs_a = [(i, i ^ 1) for i in range(NZ)]
    pairs_b = [(i, ((i + 1) ^ 1) - 1) for i in range(NZ)]
    pairs_b = [(i, j % NZ) for i, j in pairs_b]
    ring_a = [(i, i ^ 1) for i in range(4)]
    ring_b = [(i, (((i + 1) ^ 1) - 1) % 4) for i in range(4)]
    z_index = lax.axis_index(planes)
    x_index = lax.axis_index("x")
    tm_index = lax.axis_index(("yh", "c"))
    odd = jnp.stack([lax.axis_index("yl") % 2, x_index % 2]).astype(jnp.int32)

    field = eigvecs.reshape(6 * NEV, 1, SITES)
    links = gauge_links.reshape(54, 1, SITES)
    site_shape = shape((3, SITES, 128), F32)
    row_shape = shape((3, ROW, 128), F32)
    values, send_za, send_zb, send_xa, send_xb, cols = run(
        kernel_prepare,
        (site_shape, site_shape, site_shape, row_shape, row_shape, shape((SITES, 54), F32)),
        (odd, field, links),
        scalar=True,
    )
    recv_za = lax.ppermute(send_za, planes, pairs_a)
    recv_zb = lax.ppermute(send_zb, planes, pairs_b)
    recv_xa = lax.ppermute(send_xa, "x", ring_a)
    recv_xb = lax.ppermute(send_xb, "x", ring_b)

    inner = run(kernel_inner, site_shape, (values, cols))
    mine = lax.dynamic_index_in_dim(momenta.reshape(4, 4, 2, 3), x_index, 1, keepdims=False).reshape(8, 3)
    phase = phases(mine, z_index)
    factors = run(kernel_factors, shape((4, 128, 16 * 128), BF16), (perambulators.reshape(4, 2, 16, NEV, NEV),))

    send, smeared = run(
        kernel_smear,
        (shape((4, 3, SITES, 128), BF16), shape((2, 3, NEV, SITES), BF16)),
        (odd, inner, cols, recv_za, recv_zb, recv_xa, recv_xb),
        scalar=True,
    )
    shared = swap(send, "x")
    scale = 1.0 / math.sqrt(3.0 * NZ * LX * LX)

    def contract(*refs):
        kernel_contract(*refs, scale=scale)

    partial = run(
        contract,
        shape((4, 4, 32, 128), F32),
        (shared, phase),
        scratch=[pltpu.VMEM((12 * SITES, 128), F32), pltpu.VMEM((12 * SITES, 128), F32)],
    )
    pieces = swap(partial.reshape(16, 32, 128), ("zl", "yl"))
    part = jnp.sum(pieces, axis=0)
    part = jnp.sum(spread(part, "zh", 3), axis=0)
    near = spread(part.astype(BF16), ("zl", "yh", "c"), 16).reshape(4, 4, 32, 128)
    payload = run(
        kernel_correlate,
        shape((16, 144, 128), BF16),
        (tm_index.astype(jnp.int32).reshape(1), near, factors),
        scalar=True,
    )
    everything = swap(payload, ("yl", "x"))
    elementals = run(kernel_unpack, shape((32, 2, NEV, NEV), BF16), (everything,))
    terms = everything[:, 128:136, :6].astype(F32).reshape(16, 2, 4, 3, 2)
    correlator = (terms[..., 0, :] + terms[..., 1, :]) + terms[..., 2, :]
    correlator = jnp.moveaxis(correlator.reshape(32, 4, 2), 2, 0)
    return (
        smeared.reshape(1, 2, 3, NEV, 1, SITES),
        elementals.reshape(32, 1, 2, NEV, NEV),
        correlator.reshape(2, 32, 1, 4),
    )


def solution(mesh):
    fine = Mesh(mesh.devices.reshape(3, 4, 4, 4, 2, 2), ("zh", "zl", "yl", "x", "yh", "c"))
    space = ("zh", "zl", "yl", "x")
    times = ("yh", "c")

    return jax.shard_map(
        local,
        mesh=fine,
        in_specs=(
            P(times, None, None, None, space, None),
            P(None, times, None, None, None, space, None),
            P(times, None, None, None, None, None, None),
            P(),
        ),
        out_specs=(
            P(times, None, None, None, space, None),
            P(None, times, None, None, None),
            P(None, None, times, None),
        ),
        check_vma=False,
    )
```

```python
import math

import jax
import jax.numpy as jnp
from jax import lax
from jax.experimental import pallas as pl
from jax.experimental.pallas import tpu as pltpu
from jax.sharding import Mesh, PartitionSpec as P


NEV = 64
LX = 24
NZ = 48
SITES = 144
ROW = LX
KAPPA = 0.25
F32 = jnp.float32
BF16 = jnp.bfloat16
NT_DIMS = (((1,), (1,)), ((), ()))

USE_PALLAS = True


def roll(x, shift, axis):
    shift = shift % x.shape[axis]
    if USE_PALLAS:
        return pltpu.roll(x, shift, axis)
    return jnp.roll(x, shift, axis)


def half_sign(shape, low):
    lane = lax.broadcasted_iota(jnp.int32, shape, len(shape) - 1)
    return jnp.where(lane < 64, low, -low).astype(F32)


def turned(x):
    return roll(x, 64, 1) * half_sign(x.shape, -1.0)


def link(cols, mu, part, row, col, lo, hi):
    index = ((mu * 2 + part) * 3 + row) * 3 + col
    return cols[lo:hi, index : index + 1]


def carry(cols, mu, values, adjoint, lo, hi):
    spun = [turned(v) for v in values]
    out = []
    for i in range(3):
        total = None
        for j in range(3):
            if adjoint:
                term = link(cols, mu, 0, j, i, lo, hi) * values[j] - link(cols, mu, 1, j, i, lo, hi) * spun[j]
            else:
                term = link(cols, mu, 0, i, j, lo, hi) * values[j] + link(cols, mu, 1, i, j, lo, hi) * spun[j]
            total = term if total is None else total + term
        out.append(total)
    return out


def kernel_prepare(odd_ref, v_hbm, g_hbm, vt_ref, za_ref, zb_ref, xa_ref, xb_ref, cols_ref, v_ref, g_ref, sem):
    copy_g = pltpu.make_async_copy(g_hbm, g_ref, sem.at[0])
    copy_v = pltpu.make_async_copy(v_hbm, v_ref, sem.at[1])
    copy_g.start()
    copy_v.start()
    copy_g.wait()
    cols = g_ref[:, 0, :].T
    cols_ref[...] = cols
    copy_v.wait()
    values = []
    for c in range(3):
        both = jnp.concatenate([v_ref[c * 64 : (c + 1) * 64, 0, :], v_ref[192 + c * 64 : 256 + c * 64, 0, :]], axis=0)
        values.append(both.T)
    back = carry(cols, 2, values, True, 0, SITES)
    edge = carry(cols, 1, [v[SITES - ROW :] for v in values], True, SITES - ROW, SITES)
    plane_odd = odd_ref[0] == 1
    block_odd = odd_ref[1] == 1
    for c in range(3):
        vt_ref[c] = values[c]
        za_ref[c] = jnp.where(plane_odd, values[c], back[c])
        zb_ref[c] = jnp.where(plane_odd, back[c], values[c])
        xa_ref[c] = jnp.where(block_odd, values[c][:ROW], edge[c])
        xb_ref[c] = jnp.where(block_odd, edge[c], values[c][:ROW])


def kernel_inner(vt_ref, cols_ref, acc_ref):
    cols = cols_ref[...]
    values = [vt_ref[c] for c in range(3)]
    x_coord = lax.broadcasted_iota(jnp.int32, (SITES, 128), 0) % LX
    ahead = [jnp.where(x_coord == LX - 1, roll(v, LX - 1, 0), roll(v, -1, 0)) for v in values]
    fwd = carry(cols, 0, ahead, False, 0, SITES)
    back = carry(cols, 0, values, True, 0, SITES)
    back = [jnp.where(x_coord == 0, roll(b, -(LX - 1), 0), roll(b, 1, 0)) for b in back]
    up = carry(cols, 1, [v[ROW:] for v in values], False, 0, SITES - ROW)
    down = carry(cols, 1, [v[: SITES - ROW] for v in values], True, 0, SITES - ROW)
    zero = jnp.zeros((ROW, 128), F32)
    for c in range(3):
        inner_y = jnp.concatenate([up[c], zero], axis=0) + jnp.concatenate([zero, down[c]], axis=0)
        acc_ref[c] = (1.0 - 6.0 * KAPPA) * values[c] + KAPPA * (fwd[c] + back[c]) + KAPPA * inner_y


def kernel_smear(odd_ref, acc_ref, cols_ref, za_ref, zb_ref, xa_ref, xb_ref, send_ref):
    cols = cols_ref[...]
    plane_odd = odd_ref[0] == 1
    block_odd = odd_ref[1] == 1
    fwd = carry(cols, 2, [jnp.where(plane_odd, zb_ref[c], za_ref[c]) for c in range(3)], False, 0, SITES)
    edge = carry(cols, 1, [jnp.where(block_odd, xb_ref[c], xa_ref[c]) for c in range(3)], False, SITES - ROW, SITES)
    middle = jnp.zeros((SITES - 2 * ROW, 128), F32)
    for c in range(3):
        below = jnp.where(plane_odd, za_ref[c], zb_ref[c])
        row_below = jnp.where(block_odd, xa_ref[c], xb_ref[c])
        rims = jnp.concatenate([row_below, middle, edge[c]], axis=0)
        total = acc_ref[c] + KAPPA * rims + KAPPA * (fwd[c] + below)
        rounded = total.astype(BF16)
        for k in range(4):
            send_ref[k, c] = rounded


def kernel_output(s_ref, out_ref):
    for c in range(3):
        flat = s_ref[0, c].astype(F32).T
        out_ref[0, c] = flat[:64].astype(BF16)
        out_ref[1, c] = flat[64:].astype(BF16)


def kernel_contract(s_ref, ph_ref, out_ref, wide_ref, spun_ref, *, scale):
    lhs = []
    for k in range(4):
        for c in range(3):
            at = (k * 3 + c) * SITES
            wide = s_ref[k, c].astype(F32)
            wide_ref[at : at + SITES] = wide
            spun_ref[at : at + SITES] = turned(wide)
            lhs.append(wide.T.astype(BF16))
    lhs = jnp.concatenate(lhs, axis=1)
    phase = ph_ref[...].T
    sign = half_sign((64, 128), 1.0)
    for yl in range(4):
        pair = []
        for pp in range(2):
            p = yl * 2 + pp
            parts = []
            for k in range(4):
                cos = jnp.broadcast_to(phase[k * SITES : (k + 1) * SITES, p : p + 1], (SITES, 128))
                sin = jnp.broadcast_to(phase[k * SITES : (k + 1) * SITES, 8 + p : 9 + p], (SITES, 128))
                for c in range(3):
                    at = (k * 3 + c) * SITES
                    parts.append((wide_ref[at : at + SITES] * cos + spun_ref[at : at + SITES] * sin).astype(BF16))
            pair.append(jnp.concatenate(parts, axis=0))
        both = jnp.concatenate(pair, axis=1)
        prod = jnp.dot(lhs, both, preferred_element_type=F32)
        for pp in range(2):
            block = prod[:, pp * 128 : (pp + 1) * 128]
            result = (block[:64] + roll(block[64:], 64, 1) * sign) * scale
            out_ref[pp * 2, yl] = result[:32]
            out_ref[pp * 2 + 1, yl] = result[32:]


def kernel_factors(p_ref, out_ref):
    for t0 in range(4):
        for q in range(16):
            real = p_ref[t0, 0, q].astype(F32)
            imag = p_ref[t0, 1, q].astype(F32)
            at = q * 128
            out_ref[t0, :64, at : at + 128] = jnp.concatenate([real, imag], axis=1).astype(BF16)
            out_ref[t0, 64:, at : at + 128] = jnp.concatenate([-imag, real], axis=1).astype(BF16)


def kernel_correlate(tm_ref, e_ref, b_ref, out_ref):
    own = tm_ref[0]
    flip = []
    for pp in range(2):
        phi = jnp.concatenate([e_ref[2 * pp, own], e_ref[2 * pp + 1, own]], axis=0)
        for k in range(16):
            out_ref[k, pp * 64 : (pp + 1) * 64] = phi
        tall = phi.astype(F32).T
        flip.append(jnp.concatenate([tall[:64], tall[64:]], axis=1))
    sign = half_sign((64, 128), 1.0)
    row = lax.broadcasted_iota(jnp.int32, (16, 128), 0)
    lane = lax.broadcasted_iota(jnp.int32, (16, 128), 1)
    tile = jnp.zeros((16, 128), F32)
    for t0 in range(4):
        weights = []
        for pp in range(2):
            far = jnp.concatenate([e_ref[2 * pp, t0], e_ref[2 * pp + 1, t0]], axis=0)
            weights.append(far)
            weights.append(turned(far.astype(F32)).astype(BF16))
        weights = jnp.concatenate(weights, axis=0)
        first = jnp.concatenate([b_ref[t0, :64, q * 128 : (q + 1) * 128] for q in range(16)], axis=0)
        left = lax.dot_general(first, weights, NT_DIMS, preferred_element_type=F32).astype(BF16)
        tall = []
        for pp in range(2):
            tall.append(
                jnp.concatenate([left[q * 64 : (q + 1) * 64, pp * 128 : (pp + 1) * 128] for q in range(16)], axis=1)
            )
        tall = jnp.concatenate(tall, axis=0)
        right = lax.dot_general(tall, b_ref[t0], NT_DIMS, preferred_element_type=F32)
        for pp in range(2):
            block = right[pp * 64 : (pp + 1) * 64]
            real = jnp.sum(flip[pp] * block * sign) * (1.0 / NEV)
            imag = jnp.sum(flip[pp] * roll(block, 64, 1)) * (1.0 / NEV)
            tile = jnp.where((row == pp) & (lane % 8 == t0), real, tile)
            tile = jnp.where((row == pp) & (lane % 8 == 4 + t0), imag, tile)
    high = tile.astype(BF16).astype(F32)
    middle = (tile - high).astype(BF16).astype(F32)
    low = tile - high - middle
    packed = jnp.where(lane < 8, high, jnp.where(lane < 16, middle, low)).astype(BF16)
    for k in range(16):
        out_ref[k, 128:144] = packed


def kernel_unpack(r_ref, e_ref, c_ref):
    rows = jnp.concatenate([r_ref[s, 128:144].astype(F32)[:2] for s in range(16)], axis=0)
    total = (rows + roll(rows, -8, 1)) + roll(rows, -16, 1)
    tall = total.T
    c_ref[0] = tall[:4]
    c_ref[1] = tall[4:8]
    for s in range(16):
        for pp in range(2):
            both = r_ref[s, pp * 64 : (pp + 1) * 64]
            e_ref[2 * s + pp, 0] = both[:, :64]
            e_ref[2 * s + pp, 1] = both[:, 64:]


def shape(dims, dtype):
    return jax.ShapeDtypeStruct(dims, dtype)


def run(kernel, outs, args, scratch=(), scalar=False, raw=False):
    in_specs = None
    if raw:
        in_specs = [pl.BlockSpec(memory_space=pltpu.SMEM)] + [pl.BlockSpec(memory_space=pltpu.HBM)] * (len(args) - 1)
    elif scalar:
        in_specs = [pl.BlockSpec(memory_space=pltpu.SMEM)] + [pl.BlockSpec(memory_space=pltpu.VMEM)] * (len(args) - 1)
    else:
        in_specs = [pl.BlockSpec(memory_space=pltpu.VMEM)] * len(args)
    return pl.pallas_call(
        kernel,
        out_shape=outs,
        in_specs=in_specs,
        out_specs=jax.tree.map(lambda _: pl.BlockSpec(memory_space=pltpu.VMEM), outs),
        scratch_shapes=list(scratch),
        compiler_params=pltpu.CompilerParams(vmem_limit_bytes=48 << 20),
    )(*args)


def phases(momenta, z_index):
    site = jnp.arange(4 * SITES, dtype=jnp.int32)
    turn_x = momenta[:, 0, None] * (site % LX)[None] % LX
    turn_y = momenta[:, 1, None] * (site // LX)[None] % LX
    turn_z = momenta[:, 2, None] * z_index % NZ
    angles = (
        2.0
        * math.pi
        * (turn_x.astype(F32) / LX + turn_y.astype(F32) / LX + turn_z.astype(F32) / NZ)
    )
    return jnp.concatenate([jnp.cos(angles), -jnp.sin(angles)], axis=0)


def swap(value, axes):
    return lax.all_to_all(value, axes, split_axis=0, concat_axis=0, tiled=True)


def spread(value, axes, count):
    return swap(jnp.broadcast_to(value[None], (count,) + value.shape), axes)


def local(eigvecs, gauge_links, perambulators, momenta):
    planes = ("zh", "zl", "yl")
    pairs_a = [(i, i ^ 1) for i in range(NZ)]
    pairs_b = [(i, ((i + 1) ^ 1) - 1) for i in range(NZ)]
    pairs_b = [(i, j % NZ) for i, j in pairs_b]
    ring_a = [(i, i ^ 1) for i in range(4)]
    ring_b = [(i, (((i + 1) ^ 1) - 1) % 4) for i in range(4)]
    z_index = lax.axis_index(planes)
    x_index = lax.axis_index("x")
    tm_index = lax.axis_index(("yh", "c"))
    odd = jnp.stack([lax.axis_index("yl") % 2, x_index % 2]).astype(jnp.int32)

    field = eigvecs.reshape(6 * NEV, 1, SITES)
    links = gauge_links.reshape(54, 1, SITES)
    site_shape = shape((3, SITES, 128), F32)
    row_shape = shape((3, ROW, 128), F32)
    values, send_za, send_zb, send_xa, send_xb, cols = run(
        kernel_prepare,
        (site_shape, site_shape, site_shape, row_shape, row_shape, shape((SITES, 54), F32)),
        (odd, field, links),
        scratch=[
            pltpu.VMEM((6 * NEV, 1, SITES), F32),
            pltpu.VMEM((54, 1, SITES), F32),
            pltpu.SemaphoreType.DMA((2,)),
        ],
        raw=True,
    )
    recv_za = lax.ppermute(send_za, planes, pairs_a)
    recv_zb = lax.ppermute(send_zb, planes, pairs_b)
    recv_xa = lax.ppermute(send_xa, "x", ring_a)
    recv_xb = lax.ppermute(send_xb, "x", ring_b)

    inner = run(kernel_inner, site_shape, (values, cols))
    send = run(
        kernel_smear,
        shape((4, 3, SITES, 128), BF16),
        (odd, inner, cols, recv_za, recv_zb, recv_xa, recv_xb),
        scalar=True,
    )
    send, momenta, perambulators = lax.optimization_barrier((send, momenta, perambulators))
    shared = swap(send, "x")
    smeared = run(kernel_output, shape((2, 3, NEV, SITES), BF16), (send,))
    mine = lax.dynamic_index_in_dim(momenta.reshape(4, 4, 2, 3), x_index, 1, keepdims=False).reshape(8, 3)
    phase = phases(mine, z_index)
    factors = run(kernel_factors, shape((4, 128, 16 * 128), BF16), (perambulators.reshape(4, 2, 16, NEV, NEV),))

    scale = 1.0 / math.sqrt(3.0 * NZ * LX * LX)

    def contract(*refs):
        kernel_contract(*refs, scale=scale)

    partial = run(
        contract,
        shape((4, 4, 32, 128), F32),
        (shared, phase),
        scratch=[pltpu.VMEM((12 * SITES, 128), F32), pltpu.VMEM((12 * SITES, 128), F32)],
    )
    pieces = swap(partial.reshape(16, 32, 128), ("zl", "yl"))
    part = jnp.sum(pieces, axis=0)
    part = jnp.sum(spread(part, "zh", 3), axis=0)
    near = spread(part.astype(BF16), ("zl", "yh", "c"), 16).reshape(4, 4, 32, 128)
    payload = run(
        kernel_correlate,
        shape((16, 144, 128), BF16),
        (tm_index.astype(jnp.int32).reshape(1), near, factors),
        scalar=True,
    )
    everything = swap(payload, ("yl", "x"))
    elementals, correlator = run(kernel_unpack, (shape((32, 2, NEV, NEV), BF16), shape((2, 4, 32), F32)), (everything,))
    return (
        smeared.reshape(1, 2, 3, NEV, 1, SITES),
        elementals.reshape(32, 1, 2, NEV, NEV),
        jnp.swapaxes(correlator, 1, 2).reshape(2, 32, 1, 4),
    )


def solution(mesh):
    fine = Mesh(mesh.devices.reshape(3, 4, 4, 4, 2, 2), ("zh", "zl", "yl", "x", "yh", "c"))
    space = ("zh", "zl", "yl", "x")
    times = ("yh", "c")

    return jax.shard_map(
        local,
        mesh=fine,
        in_specs=(
            P(times, None, None, None, space, None),
            P(None, times, None, None, None, space, None),
            P(times, None, None, None, None, None, None),
            P(),
        ),
        out_specs=(
            P(times, None, None, None, space, None),
            P(None, times, None, None, None),
            P(None, None, times, None),
        ),
        check_vma=False,
    )
```

```python
import math

import jax
import jax.numpy as jnp
from jax import lax
from jax.experimental import pallas as pl
from jax.experimental.pallas import tpu as pltpu
from jax.sharding import Mesh, PartitionSpec as P


NEV = 64
LX = 24
NZ = 48
SITES = 144
ROW = LX
KAPPA = 0.25
F32 = jnp.float32
BF16 = jnp.bfloat16
NT_DIMS = (((1,), (1,)), ((), ()))

USE_PALLAS = True


def roll(x, shift, axis):
    shift = shift % x.shape[axis]
    if USE_PALLAS:
        return pltpu.roll(x, shift, axis)
    return jnp.roll(x, shift, axis)


def half_sign(shape, low):
    lane = lax.broadcasted_iota(jnp.int32, shape, len(shape) - 1)
    return jnp.where(lane < 64, low, -low).astype(F32)


def turned(x):
    return roll(x, 64, 1) * half_sign(x.shape, -1.0)


def link(cols, mu, part, row, col, lo, hi):
    index = ((mu * 2 + part) * 3 + row) * 3 + col
    return cols[lo:hi, index : index + 1]


def carry(cols, mu, values, adjoint, lo, hi):
    spun = [turned(v) for v in values]
    out = []
    for i in range(3):
        total = None
        for j in range(3):
            if adjoint:
                term = link(cols, mu, 0, j, i, lo, hi) * values[j] - link(cols, mu, 1, j, i, lo, hi) * spun[j]
            else:
                term = link(cols, mu, 0, i, j, lo, hi) * values[j] + link(cols, mu, 1, i, j, lo, hi) * spun[j]
            total = term if total is None else total + term
        out.append(total)
    return out


def kernel_prepare(odd_ref, v_hbm, g_hbm, vt_ref, za_ref, zb_ref, xa_ref, xb_ref, cols_ref, v_ref, g_ref, sem):
    copy_g = pltpu.make_async_copy(g_hbm, g_ref, sem.at[0])
    copy_v = pltpu.make_async_copy(v_hbm, v_ref, sem.at[1])
    copy_g.start()
    copy_v.start()
    copy_g.wait()
    cols = g_ref[:, 0, :].T
    cols_ref[...] = cols
    copy_v.wait()
    values = []
    for c in range(3):
        both = jnp.concatenate([v_ref[c * 64 : (c + 1) * 64, 0, :], v_ref[192 + c * 64 : 256 + c * 64, 0, :]], axis=0)
        values.append(both.T)
    back = carry(cols, 2, values, True, 0, SITES)
    edge = carry(cols, 1, [v[SITES - ROW :] for v in values], True, SITES - ROW, SITES)
    plane_odd = odd_ref[0] == 1
    block_odd = odd_ref[1] == 1
    for c in range(3):
        vt_ref[c] = values[c]
        za_ref[c] = jnp.where(plane_odd, values[c], back[c])
        zb_ref[c] = jnp.where(plane_odd, back[c], values[c])
        xa_ref[c] = jnp.where(block_odd, values[c][:ROW], edge[c])
        xb_ref[c] = jnp.where(block_odd, edge[c], values[c][:ROW])


def kernel_inner(vt_ref, cols_ref, acc_ref):
    cols = cols_ref[...]
    values = [vt_ref[c] for c in range(3)]
    x_coord = lax.broadcasted_iota(jnp.int32, (SITES, 128), 0) % LX
    ahead = [jnp.where(x_coord == LX - 1, roll(v, LX - 1, 0), roll(v, -1, 0)) for v in values]
    fwd = carry(cols, 0, ahead, False, 0, SITES)
    back = carry(cols, 0, values, True, 0, SITES)
    back = [jnp.where(x_coord == 0, roll(b, -(LX - 1), 0), roll(b, 1, 0)) for b in back]
    up = carry(cols, 1, [v[ROW:] for v in values], False, 0, SITES - ROW)
    down = carry(cols, 1, [v[: SITES - ROW] for v in values], True, 0, SITES - ROW)
    zero = jnp.zeros((ROW, 128), F32)
    for c in range(3):
        inner_y = jnp.concatenate([up[c], zero], axis=0) + jnp.concatenate([zero, down[c]], axis=0)
        acc_ref[c] = (1.0 - 6.0 * KAPPA) * values[c] + KAPPA * (fwd[c] + back[c]) + KAPPA * inner_y


def kernel_smear(odd_ref, acc_ref, cols_ref, za_ref, zb_ref, xa_ref, xb_ref, send_ref):
    cols = cols_ref[...]
    plane_odd = odd_ref[0] == 1
    block_odd = odd_ref[1] == 1
    fwd = carry(cols, 2, [jnp.where(plane_odd, zb_ref[c], za_ref[c]) for c in range(3)], False, 0, SITES)
    edge = carry(cols, 1, [jnp.where(block_odd, xb_ref[c], xa_ref[c]) for c in range(3)], False, SITES - ROW, SITES)
    middle = jnp.zeros((SITES - 2 * ROW, 128), F32)
    for c in range(3):
        below = jnp.where(plane_odd, za_ref[c], zb_ref[c])
        row_below = jnp.where(block_odd, xa_ref[c], xb_ref[c])
        rims = jnp.concatenate([row_below, middle, edge[c]], axis=0)
        total = acc_ref[c] + KAPPA * rims + KAPPA * (fwd[c] + below)
        rounded = total.astype(BF16)
        for k in range(4):
            send_ref[k, c] = rounded


def kernel_output(s_ref, out_ref):
    for c in range(3):
        flat = s_ref[0, c].astype(F32).T
        out_ref[0, c] = flat[:64].astype(BF16)
        out_ref[1, c] = flat[64:].astype(BF16)


def kernel_contract(s_ref, ph_ref, out_ref, wide_ref, spun_ref, lhs_ref, rhs_ref, wave_ref, *, scale):
    phase = ph_ref[...]
    high = phase.astype(BF16)
    rest = phase - high.astype(F32)
    middle = rest.astype(BF16)
    low = (rest - middle.astype(F32)).astype(BF16)
    split = jnp.concatenate([high.astype(F32), middle.astype(F32), low.astype(F32)], axis=0).T.astype(BF16)
    row = lax.broadcasted_iota(jnp.int32, (48, 256), 0) % 16
    lane = lax.broadcasted_iota(jnp.int32, (48, 256), 1) // 128

    def spread_phase(p):
        ones = jnp.where(row == p + 8 * lane, 1.0, 0.0).astype(BF16)
        wave_ref[p] = jnp.dot(split, ones, preferred_element_type=F32)

    spread_phase(0)
    for k in range(4):
        for c in range(3):
            at = (k * 3 + c) * SITES
            wide = s_ref[k, c].astype(F32)
            wide_ref[at : at + SITES] = wide
            spun_ref[at : at + SITES] = turned(wide)
            lhs_ref[:, at : at + SITES] = wide.T.astype(BF16)
    sign = half_sign((64, 128), 1.0)
    for yl in range(4):
        for pp in range(2):
            p = yl * 2 + pp
            if p < 7:
                spread_phase(p + 1)
            for k in range(4):
                for r in range(0, SITES, 16):
                    site = k * SITES + r
                    cos = wave_ref[p, site : site + 16, :128]
                    sin = wave_ref[p, site : site + 16, 128:]
                    for c in range(3):
                        at = (k * 3 + c) * SITES + r
                        value = wide_ref[at : at + 16] * cos + spun_ref[at : at + 16] * sin
                        rhs_ref[yl, at : at + 16, pp * 128 : (pp + 1) * 128] = value.astype(BF16)
        prod = jnp.dot(lhs_ref[...], rhs_ref[yl], preferred_element_type=F32)
        for pp in range(2):
            block = prod[:, pp * 128 : (pp + 1) * 128]
            result = (block[:64] + roll(block[64:], 64, 1) * sign) * scale
            out_ref[pp * 2, yl] = result[:32]
            out_ref[pp * 2 + 1, yl] = result[32:]


def kernel_factors(p_ref, out_ref):
    for t0 in range(4):
        for q in range(16):
            real = p_ref[t0, 0, q].astype(F32)
            imag = p_ref[t0, 1, q].astype(F32)
            at = q * 128
            out_ref[t0, :64, at : at + 128] = jnp.concatenate([real, imag], axis=1).astype(BF16)
            out_ref[t0, 64:, at : at + 128] = jnp.concatenate([-imag, real], axis=1).astype(BF16)


def kernel_correlate(tm_ref, e_ref, b_ref, out_ref):
    own = tm_ref[0]
    flip = []
    for pp in range(2):
        phi = jnp.concatenate([e_ref[2 * pp, own], e_ref[2 * pp + 1, own]], axis=0)
        for k in range(16):
            out_ref[k, pp * 64 : (pp + 1) * 64] = phi
        tall = phi.astype(F32).T
        flip.append(jnp.concatenate([tall[:64], tall[64:]], axis=1))
    sign = half_sign((64, 128), 1.0)
    row = lax.broadcasted_iota(jnp.int32, (16, 128), 0)
    lane = lax.broadcasted_iota(jnp.int32, (16, 128), 1)
    tile = jnp.zeros((16, 128), F32)
    for t0 in range(4):
        weights = []
        for pp in range(2):
            far = jnp.concatenate([e_ref[2 * pp, t0], e_ref[2 * pp + 1, t0]], axis=0)
            weights.append(far)
            weights.append(turned(far.astype(F32)).astype(BF16))
        weights = jnp.concatenate(weights, axis=0)
        first = jnp.concatenate([b_ref[t0, :64, q * 128 : (q + 1) * 128] for q in range(16)], axis=0)
        left = lax.dot_general(first, weights, NT_DIMS, preferred_element_type=F32).astype(BF16)
        tall = []
        for pp in range(2):
            tall.append(
                jnp.concatenate([left[q * 64 : (q + 1) * 64, pp * 128 : (pp + 1) * 128] for q in range(16)], axis=1)
            )
        tall = jnp.concatenate(tall, axis=0)
        right = lax.dot_general(tall, b_ref[t0], NT_DIMS, preferred_element_type=F32)
        for pp in range(2):
            block = right[pp * 64 : (pp + 1) * 64]
            real = jnp.sum(flip[pp] * block * sign) * (1.0 / NEV)
            imag = jnp.sum(flip[pp] * roll(block, 64, 1)) * (1.0 / NEV)
            tile = jnp.where((row == pp) & (lane % 8 == t0), real, tile)
            tile = jnp.where((row == pp) & (lane % 8 == 4 + t0), imag, tile)
    high = tile.astype(BF16).astype(F32)
    middle = (tile - high).astype(BF16).astype(F32)
    low = tile - high - middle
    packed = jnp.where(lane < 8, high, jnp.where(lane < 16, middle, low)).astype(BF16)
    for k in range(16):
        out_ref[k, 128:144] = packed


def kernel_unpack(r_ref, e_ref, c_ref):
    rows = jnp.concatenate([r_ref[s, 128:144].astype(F32)[:2] for s in range(16)], axis=0)
    total = (rows + roll(rows, -8, 1)) + roll(rows, -16, 1)
    tall = total.T
    c_ref[0] = tall[:4]
    c_ref[1] = tall[4:8]
    for s in range(16):
        for pp in range(2):
            both = r_ref[s, pp * 64 : (pp + 1) * 64]
            e_ref[2 * s + pp, 0] = both[:, :64]
            e_ref[2 * s + pp, 1] = both[:, 64:]


def shape(dims, dtype):
    return jax.ShapeDtypeStruct(dims, dtype)


def run(kernel, outs, args, scratch=(), scalar=False, raw=False):
    in_specs = None
    if raw:
        in_specs = [pl.BlockSpec(memory_space=pltpu.SMEM)] + [pl.BlockSpec(memory_space=pltpu.HBM)] * (len(args) - 1)
    elif scalar:
        in_specs = [pl.BlockSpec(memory_space=pltpu.SMEM)] + [pl.BlockSpec(memory_space=pltpu.VMEM)] * (len(args) - 1)
    else:
        in_specs = [pl.BlockSpec(memory_space=pltpu.VMEM)] * len(args)
    return pl.pallas_call(
        kernel,
        out_shape=outs,
        in_specs=in_specs,
        out_specs=jax.tree.map(lambda _: pl.BlockSpec(memory_space=pltpu.VMEM), outs),
        scratch_shapes=list(scratch),
        compiler_params=pltpu.CompilerParams(vmem_limit_bytes=48 << 20),
    )(*args)


def phases(momenta, z_index):
    site = jnp.arange(4 * SITES, dtype=jnp.int32)
    turn_x = momenta[:, 0, None] * (site % LX)[None] % LX
    turn_y = momenta[:, 1, None] * (site // LX)[None] % LX
    turn_z = momenta[:, 2, None] * z_index % NZ
    angles = (
        2.0
        * math.pi
        * (turn_x.astype(F32) / LX + turn_y.astype(F32) / LX + turn_z.astype(F32) / NZ)
    )
    return jnp.concatenate([jnp.cos(angles), -jnp.sin(angles)], axis=0)


def swap(value, axes):
    return lax.all_to_all(value, axes, split_axis=0, concat_axis=0, tiled=True)


def spread(value, axes, count):
    return swap(jnp.broadcast_to(value[None], (count,) + value.shape), axes)


def local(eigvecs, gauge_links, perambulators, momenta):
    planes = ("zh", "zl", "yl")
    pairs_a = [(i, i ^ 1) for i in range(NZ)]
    pairs_b = [(i, ((i + 1) ^ 1) - 1) for i in range(NZ)]
    pairs_b = [(i, j % NZ) for i, j in pairs_b]
    ring_a = [(i, i ^ 1) for i in range(4)]
    ring_b = [(i, (((i + 1) ^ 1) - 1) % 4) for i in range(4)]
    z_index = lax.axis_index(planes)
    x_index = lax.axis_index("x")
    tm_index = lax.axis_index(("yh", "c"))
    odd = jnp.stack([lax.axis_index("yl") % 2, x_index % 2]).astype(jnp.int32)

    field = eigvecs.reshape(6 * NEV, 1, SITES)
    links = gauge_links.reshape(54, 1, SITES)
    site_shape = shape((3, SITES, 128), F32)
    row_shape = shape((3, ROW, 128), F32)
    values, send_za, send_zb, send_xa, send_xb, cols = run(
        kernel_prepare,
        (site_shape, site_shape, site_shape, row_shape, row_shape, shape((SITES, 54), F32)),
        (
            odd,
            pltpu.with_memory_space_constraint(field, pltpu.HBM),
            pltpu.with_memory_space_constraint(links, pltpu.HBM),
        ),
        scratch=[
            pltpu.VMEM((6 * NEV, 1, SITES), F32),
            pltpu.VMEM((54, 1, SITES), F32),
            pltpu.SemaphoreType.DMA((2,)),
        ],
        raw=True,
    )
    recv_za = lax.ppermute(send_za, planes, pairs_a)
    recv_zb = lax.ppermute(send_zb, planes, pairs_b)
    recv_xa = lax.ppermute(send_xa, "x", ring_a)
    recv_xb = lax.ppermute(send_xb, "x", ring_b)

    inner = run(kernel_inner, site_shape, (values, cols))
    send = run(
        kernel_smear,
        shape((4, 3, SITES, 128), BF16),
        (odd, inner, cols, recv_za, recv_zb, recv_xa, recv_xb),
        scalar=True,
    )
    send, momenta, perambulators = lax.optimization_barrier((send, momenta, perambulators))
    shared = swap(send, "x")
    smeared = run(kernel_output, shape((2, 3, NEV, SITES), BF16), (send,))
    mine = lax.dynamic_index_in_dim(momenta.reshape(4, 4, 2, 3), x_index, 1, keepdims=False).reshape(8, 3)
    phase = phases(mine, z_index)
    factors = run(kernel_factors, shape((4, 128, 16 * 128), BF16), (perambulators.reshape(4, 2, 16, NEV, NEV),))

    scale = 1.0 / math.sqrt(3.0 * NZ * LX * LX)

    def contract(*refs):
        kernel_contract(*refs, scale=scale)

    partial = run(
        contract,
        shape((4, 4, 32, 128), F32),
        (shared, phase),
        scratch=[
            pltpu.VMEM((12 * SITES, 128), F32),
            pltpu.VMEM((12 * SITES, 128), F32),
            pltpu.VMEM((128, 12 * SITES), BF16),
            pltpu.VMEM((4, 12 * SITES, 256), BF16),
            pltpu.VMEM((8, 4 * SITES, 256), F32),
        ],
    )
    pieces = swap(partial.reshape(16, 32, 128), ("zl", "yl"))
    part = jnp.sum(pieces, axis=0)
    part = jnp.sum(spread(part, "zh", 3), axis=0)
    near = spread(part.astype(BF16), ("zl", "yh", "c"), 16).reshape(4, 4, 32, 128)
    payload = run(
        kernel_correlate,
        shape((16, 144, 128), BF16),
        (tm_index.astype(jnp.int32).reshape(1), near, factors),
        scalar=True,
    )
    everything = swap(payload, ("yl", "x"))
    elementals, correlator = run(kernel_unpack, (shape((32, 2, NEV, NEV), BF16), shape((2, 4, 32), F32)), (everything,))
    return (
        smeared.reshape(1, 2, 3, NEV, 1, SITES),
        elementals.reshape(32, 1, 2, NEV, NEV),
        jnp.swapaxes(correlator, 1, 2).reshape(2, 32, 1, 4),
    )


def solution(mesh):
    fine = Mesh(mesh.devices.reshape(3, 4, 4, 4, 2, 2), ("zh", "zl", "yl", "x", "yh", "c"))
    space = ("zh", "zl", "yl", "x")
    times = ("yh", "c")

    return jax.shard_map(
        local,
        mesh=fine,
        in_specs=(
            P(times, None, None, None, space, None),
            P(None, times, None, None, None, space, None),
            P(times, None, None, None, None, None, None),
            P(),
        ),
        out_specs=(
            P(times, None, None, None, space, None),
            P(None, times, None, None, None),
            P(None, None, times, None),
        ),
        check_vma=False,
    )
```

```python
import math

import jax
import jax.numpy as jnp
from jax import lax
from jax.experimental import pallas as pl
from jax.experimental.pallas import tpu as pltpu
from jax.sharding import Mesh, PartitionSpec as P


NEV = 64
LX = 24
NZ = 48
SITES = 144
ROW = LX
KAPPA = 0.25
F32 = jnp.float32
BF16 = jnp.bfloat16
NT_DIMS = (((1,), (1,)), ((), ()))

USE_PALLAS = True


def roll(x, shift, axis):
    shift = shift % x.shape[axis]
    if USE_PALLAS:
        return pltpu.roll(x, shift, axis)
    return jnp.roll(x, shift, axis)


def half_sign(shape, low):
    lane = lax.broadcasted_iota(jnp.int32, shape, len(shape) - 1)
    return jnp.where(lane < 64, low, -low).astype(F32)


def turned(x):
    return roll(x, 64, 1) * half_sign(x.shape, -1.0)


def link(cols, mu, part, row, col, lo, hi):
    index = ((mu * 2 + part) * 3 + row) * 3 + col
    return cols[lo:hi, index : index + 1]


def carry(cols, mu, values, adjoint, lo, hi):
    spun = [turned(v) for v in values]
    out = []
    for i in range(3):
        total = None
        for j in range(3):
            if adjoint:
                term = link(cols, mu, 0, j, i, lo, hi) * values[j] - link(cols, mu, 1, j, i, lo, hi) * spun[j]
            else:
                term = link(cols, mu, 0, i, j, lo, hi) * values[j] + link(cols, mu, 1, i, j, lo, hi) * spun[j]
            total = term if total is None else total + term
        out.append(total)
    return out


def kernel_prepare(odd_ref, v_hbm, g_hbm, vt_ref, za_ref, zb_ref, xa_ref, xb_ref, cols_ref, v_ref, g_ref, sem):
    copy_g = pltpu.make_async_copy(g_hbm, g_ref, sem.at[0])
    copy_v = pltpu.make_async_copy(v_hbm, v_ref, sem.at[1])
    copy_g.start()
    copy_v.start()
    copy_g.wait()
    cols = g_ref[:, 0, :].T
    cols_ref[...] = cols
    copy_v.wait()
    values = []
    for c in range(3):
        both = jnp.concatenate([v_ref[c * 64 : (c + 1) * 64, 0, :], v_ref[192 + c * 64 : 256 + c * 64, 0, :]], axis=0)
        values.append(both.T)
    back = carry(cols, 2, values, True, 0, SITES)
    edge = carry(cols, 1, [v[SITES - ROW :] for v in values], True, SITES - ROW, SITES)
    plane_odd = odd_ref[0] == 1
    block_odd = odd_ref[1] == 1
    for c in range(3):
        vt_ref[c] = values[c]
        za_ref[c] = jnp.where(plane_odd, values[c], back[c])
        zb_ref[c] = jnp.where(plane_odd, back[c], values[c])
        xa_ref[c] = jnp.where(block_odd, values[c][:ROW], edge[c])
        xb_ref[c] = jnp.where(block_odd, edge[c], values[c][:ROW])


def kernel_inner(vt_ref, cols_ref, acc_ref):
    cols = cols_ref[...]
    values = [vt_ref[c] for c in range(3)]
    x_coord = lax.broadcasted_iota(jnp.int32, (SITES, 128), 0) % LX
    ahead = [jnp.where(x_coord == LX - 1, roll(v, LX - 1, 0), roll(v, -1, 0)) for v in values]
    fwd = carry(cols, 0, ahead, False, 0, SITES)
    back = carry(cols, 0, values, True, 0, SITES)
    back = [jnp.where(x_coord == 0, roll(b, -(LX - 1), 0), roll(b, 1, 0)) for b in back]
    up = carry(cols, 1, [v[ROW:] for v in values], False, 0, SITES - ROW)
    down = carry(cols, 1, [v[: SITES - ROW] for v in values], True, 0, SITES - ROW)
    zero = jnp.zeros((ROW, 128), F32)
    for c in range(3):
        inner_y = jnp.concatenate([up[c], zero], axis=0) + jnp.concatenate([zero, down[c]], axis=0)
        acc_ref[c] = (1.0 - 6.0 * KAPPA) * values[c] + KAPPA * (fwd[c] + back[c]) + KAPPA * inner_y


def kernel_smear(odd_ref, acc_ref, cols_ref, za_ref, zb_ref, xa_ref, xb_ref, send_ref):
    cols = cols_ref[...]
    plane_odd = odd_ref[0] == 1
    block_odd = odd_ref[1] == 1
    fwd = carry(cols, 2, [jnp.where(plane_odd, zb_ref[c], za_ref[c]) for c in range(3)], False, 0, SITES)
    edge = carry(cols, 1, [jnp.where(block_odd, xb_ref[c], xa_ref[c]) for c in range(3)], False, SITES - ROW, SITES)
    middle = jnp.zeros((SITES - 2 * ROW, 128), F32)
    for c in range(3):
        below = jnp.where(plane_odd, za_ref[c], zb_ref[c])
        row_below = jnp.where(block_odd, xa_ref[c], xb_ref[c])
        rims = jnp.concatenate([row_below, middle, edge[c]], axis=0)
        total = acc_ref[c] + KAPPA * rims + KAPPA * (fwd[c] + below)
        rounded = total.astype(BF16)
        for k in range(4):
            send_ref[k, c] = rounded


def kernel_output(s_ref, out_ref):
    for c in range(3):
        flat = s_ref[0, c].astype(F32).T
        out_ref[0, c] = flat[:64].astype(BF16)
        out_ref[1, c] = flat[64:].astype(BF16)


def kernel_contract(s_ref, ph_ref, out_ref, wide_ref, spun_ref, lhs_ref, rhs_ref, wave_ref, *, scale):
    phase = ph_ref[...]
    high = phase.astype(BF16)
    rest = phase - high.astype(F32)
    middle = rest.astype(BF16)
    low = (rest - middle.astype(F32)).astype(BF16)
    split = jnp.concatenate([high.astype(F32), middle.astype(F32), low.astype(F32)], axis=0).T.astype(BF16)
    row = lax.broadcasted_iota(jnp.int32, (48, 256), 0) % 16
    lane = lax.broadcasted_iota(jnp.int32, (48, 256), 1) // 128

    def spread_phase(p):
        ones = jnp.where(row == p + 8 * lane, 1.0, 0.0).astype(BF16)
        wave_ref[p] = jnp.dot(split, ones, preferred_element_type=F32)

    spread_phase(0)
    for k in range(4):
        for c in range(3):
            at = (k * 3 + c) * SITES
            wide = s_ref[k, c].astype(F32)
            wide_ref[at : at + SITES] = wide
            spun_ref[at : at + SITES] = turned(wide)
            lhs_ref[:, at : at + SITES] = wide.T.astype(BF16)
    sign = half_sign((64, 128), 1.0)
    for yl in range(4):
        for pp in range(2):
            p = yl * 2 + pp
            if p < 7:
                spread_phase(p + 1)
            for k in range(4):
                for r in range(0, SITES, 16):
                    site = k * SITES + r
                    cos = wave_ref[p, site : site + 16, :128]
                    sin = wave_ref[p, site : site + 16, 128:]
                    for c in range(3):
                        at = (k * 3 + c) * SITES + r
                        value = wide_ref[at : at + 16] * cos + spun_ref[at : at + 16] * sin
                        rhs_ref[yl, at : at + 16, pp * 128 : (pp + 1) * 128] = value.astype(BF16)
        prod = jnp.dot(lhs_ref[...], rhs_ref[yl], preferred_element_type=F32)
        for pp in range(2):
            block = prod[:, pp * 128 : (pp + 1) * 128]
            result = (block[:64] + roll(block[64:], 64, 1) * sign) * scale
            out_ref[pp * 2, yl] = result[:32]
            out_ref[pp * 2 + 1, yl] = result[32:]


def kernel_factors(p_ref, out_ref):
    for t0 in range(4):
        for q in range(16):
            real = p_ref[t0, 0, q].astype(F32)
            imag = p_ref[t0, 1, q].astype(F32)
            at = q * 128
            out_ref[t0, :64, at : at + 128] = jnp.concatenate([real, imag], axis=1).astype(BF16)
            out_ref[t0, 64:, at : at + 128] = jnp.concatenate([-imag, real], axis=1).astype(BF16)


def kernel_correlate(tm_ref, e_ref, b_ref, out_ref):
    own = tm_ref[0]
    flip = []
    for pp in range(2):
        phi = jnp.concatenate([e_ref[2 * pp, own], e_ref[2 * pp + 1, own]], axis=0)
        for k in range(16):
            out_ref[k, pp * 64 : (pp + 1) * 64] = phi
        tall = phi.astype(F32).T
        flip.append(jnp.concatenate([tall[:64], tall[64:]], axis=1))
    sign = half_sign((64, 128), 1.0)
    row = lax.broadcasted_iota(jnp.int32, (16, 128), 0)
    lane = lax.broadcasted_iota(jnp.int32, (16, 128), 1)
    tile = jnp.zeros((16, 128), F32)
    for t0 in range(4):
        weights = []
        for pp in range(2):
            far = jnp.concatenate([e_ref[2 * pp, t0], e_ref[2 * pp + 1, t0]], axis=0)
            weights.append(far)
            weights.append(turned(far.astype(F32)).astype(BF16))
        weights = jnp.concatenate(weights, axis=0)
        first = jnp.concatenate([b_ref[t0, :64, q * 128 : (q + 1) * 128] for q in range(16)], axis=0)
        left = lax.dot_general(first, weights, NT_DIMS, preferred_element_type=F32).astype(BF16)
        tall = []
        for pp in range(2):
            tall.append(
                jnp.concatenate([left[q * 64 : (q + 1) * 64, pp * 128 : (pp + 1) * 128] for q in range(16)], axis=1)
            )
        tall = jnp.concatenate(tall, axis=0)
        right = lax.dot_general(tall, b_ref[t0], NT_DIMS, preferred_element_type=F32)
        for pp in range(2):
            block = right[pp * 64 : (pp + 1) * 64]
            real = jnp.sum(flip[pp] * block * sign) * (1.0 / NEV)
            imag = jnp.sum(flip[pp] * roll(block, 64, 1)) * (1.0 / NEV)
            tile = jnp.where((row == pp) & (lane % 8 == t0), real, tile)
            tile = jnp.where((row == pp) & (lane % 8 == 4 + t0), imag, tile)
    high = tile.astype(BF16).astype(F32)
    middle = (tile - high).astype(BF16).astype(F32)
    low = tile - high - middle
    packed = jnp.where(lane < 8, high, jnp.where(lane < 16, middle, low)).astype(BF16)
    for k in range(16):
        out_ref[k, 128:144] = packed


def kernel_unpack(r_ref, e_ref, c_ref):
    rows = jnp.concatenate([r_ref[s, 128:144].astype(F32)[:2] for s in range(16)], axis=0)
    total = (rows + roll(rows, -8, 1)) + roll(rows, -16, 1)
    tall = total.T
    c_ref[0] = tall[:4]
    c_ref[1] = tall[4:8]
    for s in range(16):
        for pp in range(2):
            both = r_ref[s, pp * 64 : (pp + 1) * 64]
            e_ref[2 * s + pp, 0] = both[:, :64]
            e_ref[2 * s + pp, 1] = both[:, 64:]


def shape(dims, dtype):
    return jax.ShapeDtypeStruct(dims, dtype)


def run(kernel, outs, args, scratch=(), scalar=False, raw=False):
    in_specs = None
    if raw:
        in_specs = [pl.BlockSpec(memory_space=pltpu.SMEM)] + [pl.BlockSpec(memory_space=pltpu.HBM)] * (len(args) - 1)
    elif scalar:
        in_specs = [pl.BlockSpec(memory_space=pltpu.SMEM)] + [pl.BlockSpec(memory_space=pltpu.VMEM)] * (len(args) - 1)
    else:
        in_specs = [pl.BlockSpec(memory_space=pltpu.VMEM)] * len(args)
    return pl.pallas_call(
        kernel,
        out_shape=outs,
        in_specs=in_specs,
        out_specs=jax.tree.map(lambda _: pl.BlockSpec(memory_space=pltpu.VMEM), outs),
        scratch_shapes=list(scratch),
        compiler_params=pltpu.CompilerParams(vmem_limit_bytes=48 << 20),
    )(*args)


def phases(momenta, z_index):
    site = jnp.arange(4 * SITES, dtype=jnp.int32)
    turn_x = momenta[:, 0, None] * (site % LX)[None] % LX
    turn_y = momenta[:, 1, None] * (site // LX)[None] % LX
    turn_z = momenta[:, 2, None] * z_index % NZ
    angles = (
        2.0
        * math.pi
        * (turn_x.astype(F32) / LX + turn_y.astype(F32) / LX + turn_z.astype(F32) / NZ)
    )
    return jnp.concatenate([jnp.cos(angles), -jnp.sin(angles)], axis=0)


def swap(value, axes):
    return lax.all_to_all(value, axes, split_axis=0, concat_axis=0, tiled=True)


def spread(value, axes, count):
    return swap(jnp.broadcast_to(value[None], (count,) + value.shape), axes)


def local(eigvecs, gauge_links, perambulators, momenta):
    planes = ("zh", "zl", "yl")
    pairs_a = [(i, i ^ 1) for i in range(NZ)]
    pairs_b = [(i, ((i + 1) ^ 1) - 1) for i in range(NZ)]
    pairs_b = [(i, j % NZ) for i, j in pairs_b]
    ring_a = [(i, i ^ 1) for i in range(4)]
    ring_b = [(i, (((i + 1) ^ 1) - 1) % 4) for i in range(4)]
    z_index = lax.axis_index(planes)
    x_index = lax.axis_index("x")
    tm_index = lax.axis_index(("yh", "c"))
    odd = jnp.stack([lax.axis_index("yl") % 2, x_index % 2]).astype(jnp.int32)

    field = eigvecs.reshape(6 * NEV, 1, SITES)
    links = gauge_links.reshape(54, 1, SITES)
    site_shape = shape((3, SITES, 128), F32)
    row_shape = shape((3, ROW, 128), F32)
    values, send_za, send_zb, send_xa, send_xb, cols = run(
        kernel_prepare,
        (site_shape, site_shape, site_shape, row_shape, row_shape, shape((SITES, 54), F32)),
        (
            odd,
            pltpu.with_memory_space_constraint(field, pltpu.HBM),
            pltpu.with_memory_space_constraint(links, pltpu.HBM),
        ),
        scratch=[
            pltpu.VMEM((6 * NEV, 1, SITES), F32),
            pltpu.VMEM((54, 1, SITES), F32),
            pltpu.SemaphoreType.DMA((2,)),
        ],
        raw=True,
    )
    recv_za = lax.ppermute(send_za, planes, pairs_a)
    recv_zb = lax.ppermute(send_zb, planes, pairs_b)
    recv_xa = lax.ppermute(send_xa, "x", ring_a)
    recv_xb = lax.ppermute(send_xb, "x", ring_b)

    inner = run(kernel_inner, site_shape, (values, cols))
    send = run(
        kernel_smear,
        shape((4, 3, SITES, 128), BF16),
        (odd, inner, cols, recv_za, recv_zb, recv_xa, recv_xb),
        scalar=True,
    )
    mine = lax.dynamic_index_in_dim(momenta.reshape(4, 4, 2, 3), x_index, 1, keepdims=False).reshape(8, 3)
    phase = phases(mine, z_index)
    send, phase = lax.optimization_barrier((send, phase))
    shared = swap(send, "x")
    scale = 1.0 / math.sqrt(3.0 * NZ * LX * LX)

    def contract(*refs):
        kernel_contract(*refs, scale=scale)

    partial = run(
        contract,
        shape((4, 4, 32, 128), F32),
        (shared, phase),
        scratch=[
            pltpu.VMEM((12 * SITES, 128), F32),
            pltpu.VMEM((12 * SITES, 128), F32),
            pltpu.VMEM((128, 12 * SITES), BF16),
            pltpu.VMEM((4, 12 * SITES, 256), BF16),
            pltpu.VMEM((8, 4 * SITES, 256), F32),
        ],
    )
    pieces = swap(partial.reshape(16, 32, 128), ("zl", "yl"))
    part = jnp.sum(pieces, axis=0)
    part = jnp.sum(spread(part, "zh", 3), axis=0)
    part, perambulators, send = lax.optimization_barrier((part.astype(BF16), perambulators, send))
    near = spread(part, ("zl", "yh", "c"), 16).reshape(4, 4, 32, 128)
    factors = run(kernel_factors, shape((4, 128, 16 * 128), BF16), (perambulators.reshape(4, 2, 16, NEV, NEV),))

    smeared = run(kernel_output, shape((2, 3, NEV, SITES), BF16), (send,))
    payload = run(
        kernel_correlate,
        shape((16, 144, 128), BF16),
        (tm_index.astype(jnp.int32).reshape(1), near, factors),
        scalar=True,
    )
    payload, smeared = lax.optimization_barrier((payload, smeared))
    everything = swap(payload, ("yl", "x"))
    elementals, correlator = run(kernel_unpack, (shape((32, 2, NEV, NEV), BF16), shape((2, 4, 32), F32)), (everything,))
    return (
        smeared.reshape(1, 2, 3, NEV, 1, SITES),
        elementals.reshape(32, 1, 2, NEV, NEV),
        jnp.swapaxes(correlator, 1, 2).reshape(2, 32, 1, 4),
    )


def solution(mesh):
    fine = Mesh(mesh.devices.reshape(3, 4, 4, 4, 2, 2), ("zh", "zl", "yl", "x", "yh", "c"))
    space = ("zh", "zl", "yl", "x")
    times = ("yh", "c")

    return jax.shard_map(
        local,
        mesh=fine,
        in_specs=(
            P(times, None, None, None, space, None),
            P(None, times, None, None, None, space, None),
            P(times, None, None, None, None, None, None),
            P(),
        ),
        out_specs=(
            P(times, None, None, None, space, None),
            P(None, times, None, None, None),
            P(None, None, times, None),
        ),
        check_vma=False,
    )
```

```python
import math

import jax
import jax.numpy as jnp
from jax import lax
from jax.experimental import pallas as pl
from jax.experimental.pallas import tpu as pltpu
from jax.sharding import Mesh, PartitionSpec as P


NEV = 64
LX = 24
NZ = 48
SITES = 144
ROW = LX
KAPPA = 0.25
F32 = jnp.float32
BF16 = jnp.bfloat16
NT_DIMS = (((1,), (1,)), ((), ()))

USE_PALLAS = True


def roll(x, shift, axis):
    shift = shift % x.shape[axis]
    if USE_PALLAS:
        return pltpu.roll(x, shift, axis)
    return jnp.roll(x, shift, axis)


def half_sign(shape, low):
    lane = lax.broadcasted_iota(jnp.int32, shape, len(shape) - 1)
    return jnp.where(lane < 64, low, -low).astype(F32)


def turned(x):
    return roll(x, 64, 1) * half_sign(x.shape, -1.0)


def link(cols, mu, part, row, col, lo, hi):
    index = ((mu * 2 + part) * 3 + row) * 3 + col
    return cols[lo:hi, index : index + 1]


def carry(cols, mu, values, adjoint, lo, hi):
    spun = [turned(v) for v in values]
    out = []
    for i in range(3):
        total = None
        for j in range(3):
            if adjoint:
                term = link(cols, mu, 0, j, i, lo, hi) * values[j] - link(cols, mu, 1, j, i, lo, hi) * spun[j]
            else:
                term = link(cols, mu, 0, i, j, lo, hi) * values[j] + link(cols, mu, 1, i, j, lo, hi) * spun[j]
            total = term if total is None else total + term
        out.append(total)
    return out


def kernel_prepare(odd_ref, v_hbm, g_hbm, vt_ref, za_ref, zb_ref, xa_ref, xb_ref, cols_ref, v_ref, g_ref, sem):
    copy_g = pltpu.make_async_copy(g_hbm, g_ref, sem.at[0])
    copy_v = pltpu.make_async_copy(v_hbm, v_ref, sem.at[1])
    copy_g.start()
    copy_v.start()
    copy_g.wait()
    cols = g_ref[:, 0, :].T
    cols_ref[...] = cols
    copy_v.wait()
    values = []
    for c in range(3):
        both = jnp.concatenate([v_ref[c * 64 : (c + 1) * 64, 0, :], v_ref[192 + c * 64 : 256 + c * 64, 0, :]], axis=0)
        values.append(both.T)
    back = carry(cols, 2, values, True, 0, SITES)
    edge = carry(cols, 1, [v[SITES - ROW :] for v in values], True, SITES - ROW, SITES)
    plane_odd = odd_ref[0] == 1
    block_odd = odd_ref[1] == 1
    for c in range(3):
        vt_ref[c] = values[c]
        za_ref[c] = jnp.where(plane_odd, values[c], back[c])
        zb_ref[c] = jnp.where(plane_odd, back[c], values[c])
        xa_ref[c] = jnp.where(block_odd, values[c][:ROW], edge[c])
        xb_ref[c] = jnp.where(block_odd, edge[c], values[c][:ROW])


def kernel_inner(vt_ref, cols_ref, acc_ref):
    cols = cols_ref[...]
    values = [vt_ref[c] for c in range(3)]
    x_coord = lax.broadcasted_iota(jnp.int32, (SITES, 128), 0) % LX
    ahead = [jnp.where(x_coord == LX - 1, roll(v, LX - 1, 0), roll(v, -1, 0)) for v in values]
    fwd = carry(cols, 0, ahead, False, 0, SITES)
    back = carry(cols, 0, values, True, 0, SITES)
    back = [jnp.where(x_coord == 0, roll(b, -(LX - 1), 0), roll(b, 1, 0)) for b in back]
    up = carry(cols, 1, [v[ROW:] for v in values], False, 0, SITES - ROW)
    down = carry(cols, 1, [v[: SITES - ROW] for v in values], True, 0, SITES - ROW)
    zero = jnp.zeros((ROW, 128), F32)
    for c in range(3):
        inner_y = jnp.concatenate([up[c], zero], axis=0) + jnp.concatenate([zero, down[c]], axis=0)
        acc_ref[c] = (1.0 - 6.0 * KAPPA) * values[c] + KAPPA * (fwd[c] + back[c]) + KAPPA * inner_y


def kernel_smear(odd_ref, acc_ref, cols_ref, za_ref, zb_ref, xa_ref, xb_ref, send_ref):
    cols = cols_ref[...]
    plane_odd = odd_ref[0] == 1
    block_odd = odd_ref[1] == 1
    fwd = carry(cols, 2, [jnp.where(plane_odd, zb_ref[c], za_ref[c]) for c in range(3)], False, 0, SITES)
    edge = carry(cols, 1, [jnp.where(block_odd, xb_ref[c], xa_ref[c]) for c in range(3)], False, SITES - ROW, SITES)
    middle = jnp.zeros((SITES - 2 * ROW, 128), F32)
    for c in range(3):
        below = jnp.where(plane_odd, za_ref[c], zb_ref[c])
        row_below = jnp.where(block_odd, xa_ref[c], xb_ref[c])
        rims = jnp.concatenate([row_below, middle, edge[c]], axis=0)
        total = acc_ref[c] + KAPPA * rims + KAPPA * (fwd[c] + below)
        rounded = total.astype(BF16)
        for k in range(4):
            send_ref[k, c] = rounded


def kernel_output(s_ref, out_ref):
    for c in range(3):
        flat = s_ref[0, c].astype(F32).T
        out_ref[0, c] = flat[:64].astype(BF16)
        out_ref[1, c] = flat[64:].astype(BF16)


def kernel_contract(s_ref, ph_ref, out_ref, wide_ref, spun_ref, lhs_ref, rhs_ref, wave_ref, *, scale):
    phase = ph_ref[...]
    high = phase.astype(BF16)
    rest = phase - high.astype(F32)
    middle = rest.astype(BF16)
    low = (rest - middle.astype(F32)).astype(BF16)
    split = jnp.concatenate([high.astype(F32), middle.astype(F32), low.astype(F32)], axis=0).T.astype(BF16)
    row = lax.broadcasted_iota(jnp.int32, (48, 256), 0) % 16
    lane = lax.broadcasted_iota(jnp.int32, (48, 256), 1) // 128

    def spread_phase(p):
        ones = jnp.where(row == p + 8 * lane, 1.0, 0.0).astype(BF16)
        wave_ref[p] = jnp.dot(split, ones, preferred_element_type=F32)

    spread_phase(0)
    for k in range(4):
        for c in range(3):
            at = (k * 3 + c) * SITES
            wide = s_ref[k, c].astype(F32)
            wide_ref[at : at + SITES] = wide
            spun_ref[at : at + SITES] = turned(wide)
            lhs_ref[:, at : at + SITES] = wide.T.astype(BF16)
    sign = half_sign((64, 128), 1.0)
    for pair in range(4):
        for pp in range(2):
            p = pair * 2 + pp
            if p < 7:
                spread_phase(p + 1)
            for k in range(4):
                for r in range(0, SITES, 16):
                    site = k * SITES + r
                    cos = wave_ref[p, site : site + 16, :128]
                    sin = wave_ref[p, site : site + 16, 128:]
                    for c in range(3):
                        at = (k * 3 + c) * SITES + r
                        value = wide_ref[at : at + 16] * cos + spun_ref[at : at + 16] * sin
                        rhs_ref[pair, at : at + 16, pp * 128 : (pp + 1) * 128] = value.astype(BF16)
        prod = jnp.dot(lhs_ref[...], rhs_ref[pair], preferred_element_type=F32)
        for pp in range(2):
            block = prod[:, pp * 128 : (pp + 1) * 128]
            result = (block[:64] + roll(block[64:], 64, 1) * sign) * scale
            out_ref[pair, pp * 2] = result[:32]
            out_ref[pair, pp * 2 + 1] = result[32:]


def kernel_factors(p_ref, out_ref):
    for t0 in range(4):
        for q in range(16):
            real = p_ref[t0, 0, q].astype(F32)
            imag = p_ref[t0, 1, q].astype(F32)
            at = q * 128
            out_ref[t0, :64, at : at + 128] = jnp.concatenate([real, imag], axis=1).astype(BF16)
            out_ref[t0, 64:, at : at + 128] = jnp.concatenate([-imag, real], axis=1).astype(BF16)


def kernel_correlate(tm_ref, e_ref, b_ref, out_ref):
    own = tm_ref[0]
    flip = []
    for pp in range(2):
        phi = jnp.concatenate([e_ref[2 * pp, own], e_ref[2 * pp + 1, own]], axis=0)
        for k in range(16):
            out_ref[k, pp * 64 : (pp + 1) * 64] = phi
        tall = phi.astype(F32).T
        flip.append(jnp.concatenate([tall[:64], tall[64:]], axis=1))
    sign = half_sign((64, 128), 1.0)
    row = lax.broadcasted_iota(jnp.int32, (16, 128), 0)
    lane = lax.broadcasted_iota(jnp.int32, (16, 128), 1)
    tile = jnp.zeros((16, 128), F32)
    for t0 in range(4):
        weights = []
        for pp in range(2):
            far = jnp.concatenate([e_ref[2 * pp, t0], e_ref[2 * pp + 1, t0]], axis=0)
            weights.append(far)
            weights.append(turned(far.astype(F32)).astype(BF16))
        weights = jnp.concatenate(weights, axis=0)
        first = jnp.concatenate([b_ref[t0, :64, q * 128 : (q + 1) * 128] for q in range(16)], axis=0)
        left = lax.dot_general(first, weights, NT_DIMS, preferred_element_type=F32).astype(BF16)
        tall = []
        for pp in range(2):
            tall.append(
                jnp.concatenate([left[q * 64 : (q + 1) * 64, pp * 128 : (pp + 1) * 128] for q in range(16)], axis=1)
            )
        tall = jnp.concatenate(tall, axis=0)
        right = lax.dot_general(tall, b_ref[t0], NT_DIMS, preferred_element_type=F32)
        for pp in range(2):
            block = right[pp * 64 : (pp + 1) * 64]
            real = jnp.sum(flip[pp] * block * sign) * (1.0 / NEV)
            imag = jnp.sum(flip[pp] * roll(block, 64, 1)) * (1.0 / NEV)
            tile = jnp.where((row == pp) & (lane % 8 == t0), real, tile)
            tile = jnp.where((row == pp) & (lane % 8 == 4 + t0), imag, tile)
    high = tile.astype(BF16).astype(F32)
    middle = (tile - high).astype(BF16).astype(F32)
    low = tile - high - middle
    packed = jnp.where(lane < 8, high, jnp.where(lane < 16, middle, low)).astype(BF16)
    for k in range(16):
        out_ref[k, 128:144] = packed


def kernel_unpack(r_ref, e_ref, c_ref):
    rows = jnp.concatenate([r_ref[s, 128:144].astype(F32)[:2] for s in range(16)], axis=0)
    total = (rows + roll(rows, -8, 1)) + roll(rows, -16, 1)
    tall = total.T
    c_ref[0] = tall[:4]
    c_ref[1] = tall[4:8]
    for s in range(16):
        for pp in range(2):
            both = r_ref[s, pp * 64 : (pp + 1) * 64]
            e_ref[2 * s + pp, 0] = both[:, :64]
            e_ref[2 * s + pp, 1] = both[:, 64:]


def shape(dims, dtype):
    return jax.ShapeDtypeStruct(dims, dtype)


def run(kernel, outs, args, scratch=(), scalar=False, raw=False):
    in_specs = None
    if raw:
        in_specs = [pl.BlockSpec(memory_space=pltpu.SMEM)] + [pl.BlockSpec(memory_space=pltpu.HBM)] * (len(args) - 1)
    elif scalar:
        in_specs = [pl.BlockSpec(memory_space=pltpu.SMEM)] + [pl.BlockSpec(memory_space=pltpu.VMEM)] * (len(args) - 1)
    else:
        in_specs = [pl.BlockSpec(memory_space=pltpu.VMEM)] * len(args)
    return pl.pallas_call(
        kernel,
        out_shape=outs,
        in_specs=in_specs,
        out_specs=jax.tree.map(lambda _: pl.BlockSpec(memory_space=pltpu.VMEM), outs),
        scratch_shapes=list(scratch),
        compiler_params=pltpu.CompilerParams(vmem_limit_bytes=48 << 20),
    )(*args)


def phases(momenta, z_index):
    site = jnp.arange(4 * SITES, dtype=jnp.int32)
    turn_x = momenta[:, 0, None] * (site % LX)[None] % LX
    turn_y = momenta[:, 1, None] * (site // LX)[None] % LX
    turn_z = momenta[:, 2, None] * z_index % NZ
    angles = (
        2.0
        * math.pi
        * (turn_x.astype(F32) / LX + turn_y.astype(F32) / LX + turn_z.astype(F32) / NZ)
    )
    return jnp.concatenate([jnp.cos(angles), -jnp.sin(angles)], axis=0)


def swap(value, axes):
    return lax.all_to_all(value, axes, split_axis=0, concat_axis=0, tiled=True)


def spread(value, axes, count):
    return swap(jnp.broadcast_to(value[None], (count,) + value.shape), axes)


def local(eigvecs, gauge_links, perambulators, momenta):
    planes = ("zh", "zl", "yl")
    pairs_a = [(i, i ^ 1) for i in range(NZ)]
    pairs_b = [(i, ((i + 1) ^ 1) - 1) for i in range(NZ)]
    pairs_b = [(i, j % NZ) for i, j in pairs_b]
    ring_a = [(i, i ^ 1) for i in range(4)]
    ring_b = [(i, (((i + 1) ^ 1) - 1) % 4) for i in range(4)]
    z_index = lax.axis_index(planes)
    x_index = lax.axis_index("x")
    tm_index = lax.axis_index(("yh", "c"))
    odd = jnp.stack([lax.axis_index("yl") % 2, x_index % 2]).astype(jnp.int32)

    field = eigvecs.reshape(6 * NEV, 1, SITES)
    links = gauge_links.reshape(54, 1, SITES)
    site_shape = shape((3, SITES, 128), F32)
    row_shape = shape((3, ROW, 128), F32)
    values, send_za, send_zb, send_xa, send_xb, cols = run(
        kernel_prepare,
        (site_shape, site_shape, site_shape, row_shape, row_shape, shape((SITES, 54), F32)),
        (
            odd,
            pltpu.with_memory_space_constraint(field, pltpu.HBM),
            pltpu.with_memory_space_constraint(links, pltpu.HBM),
        ),
        scratch=[
            pltpu.VMEM((6 * NEV, 1, SITES), F32),
            pltpu.VMEM((54, 1, SITES), F32),
            pltpu.SemaphoreType.DMA((2,)),
        ],
        raw=True,
    )
    recv_za = lax.ppermute(send_za, planes, pairs_a)
    recv_zb = lax.ppermute(send_zb, planes, pairs_b)
    recv_xa = lax.ppermute(send_xa, "x", ring_a)
    recv_xb = lax.ppermute(send_xb, "x", ring_b)

    inner = run(kernel_inner, site_shape, (values, cols))
    send = run(
        kernel_smear,
        shape((4, 3, SITES, 128), BF16),
        (odd, inner, cols, recv_za, recv_zb, recv_xa, recv_xb),
        scalar=True,
    )
    mine = lax.dynamic_index_in_dim(momenta.reshape(4, 4, 2, 3), x_index, 1, keepdims=False).reshape(8, 3)
    phase = phases(mine, z_index)
    send, phase = lax.optimization_barrier((send, phase))
    shared = swap(send, "x")
    scale = 1.0 / math.sqrt(3.0 * NZ * LX * LX)

    def contract(*refs):
        kernel_contract(*refs, scale=scale)

    partial = run(
        contract,
        shape((4, 4, 32, 128), F32),
        (shared, phase),
        scratch=[
            pltpu.VMEM((12 * SITES, 128), F32),
            pltpu.VMEM((12 * SITES, 128), F32),
            pltpu.VMEM((128, 12 * SITES), BF16),
            pltpu.VMEM((4, 12 * SITES, 256), BF16),
            pltpu.VMEM((8, 4 * SITES, 256), F32),
        ],
    )
    pieces = swap(partial.reshape(16, 32, 128), ("zl", "yl"))
    part = jnp.sum(pieces, axis=0)
    part = jnp.sum(spread(part, "zh", 3), axis=0)
    part, perambulators, send = lax.optimization_barrier((part.astype(BF16), perambulators, send))
    near = spread(part, ("yl", "yh", "c"), 16).reshape(4, 4, 32, 128)
    factors = run(kernel_factors, shape((4, 128, 16 * 128), BF16), (perambulators.reshape(4, 2, 16, NEV, NEV),))

    smeared = run(kernel_output, shape((2, 3, NEV, SITES), BF16), (send,))
    payload = run(
        kernel_correlate,
        shape((16, 144, 128), BF16),
        (tm_index.astype(jnp.int32).reshape(1), near, factors),
        scalar=True,
    )
    payload, smeared = lax.optimization_barrier((payload, smeared))
    everything = swap(payload, ("zl", "x"))
    elementals, correlator = run(kernel_unpack, (shape((32, 2, NEV, NEV), BF16), shape((2, 4, 32), F32)), (everything,))
    return (
        smeared.reshape(1, 2, 3, NEV, 1, SITES),
        elementals.reshape(32, 1, 2, NEV, NEV),
        jnp.swapaxes(correlator, 1, 2).reshape(2, 32, 1, 4),
    )


def solution(mesh):
    fine = Mesh(mesh.devices.reshape(3, 4, 4, 4, 2, 2), ("zh", "zl", "yl", "x", "yh", "c"))
    space = ("zh", "zl", "yl", "x")
    times = ("yh", "c")

    return jax.shard_map(
        local,
        mesh=fine,
        in_specs=(
            P(times, None, None, None, space, None),
            P(None, times, None, None, None, space, None),
            P(times, None, None, None, None, None, None),
            P(),
        ),
        out_specs=(
            P(times, None, None, None, space, None),
            P(None, times, None, None, None),
            P(None, None, times, None),
        ),
        check_vma=False,
    )
```

```python
import math

import jax
import jax.numpy as jnp
from jax import lax
from jax.experimental import pallas as pl
from jax.experimental.pallas import tpu as pltpu
from jax.sharding import Mesh, PartitionSpec as P


NEV = 64
LX = 24
NZ = 48
SITES = 144
ROW = LX
KAPPA = 0.25
F32 = jnp.float32
BF16 = jnp.bfloat16
NT_DIMS = (((1,), (1,)), ((), ()))

USE_PALLAS = True


def roll(x, shift, axis):
    shift = shift % x.shape[axis]
    if USE_PALLAS:
        return pltpu.roll(x, shift, axis)
    return jnp.roll(x, shift, axis)


def half_sign(shape, low):
    lane = lax.broadcasted_iota(jnp.int32, shape, len(shape) - 1)
    return jnp.where(lane < 64, low, -low).astype(F32)


def turned(x):
    return roll(x, 64, 1) * half_sign(x.shape, -1.0)


def link(cols, mu, part, row, col, lo, hi):
    index = ((mu * 2 + part) * 3 + row) * 3 + col
    return cols[lo:hi, index : index + 1]


def carry(cols, mu, values, adjoint, lo, hi):
    spun = [turned(v) for v in values]
    out = []
    for i in range(3):
        total = None
        for j in range(3):
            if adjoint:
                term = link(cols, mu, 0, j, i, lo, hi) * values[j] - link(cols, mu, 1, j, i, lo, hi) * spun[j]
            else:
                term = link(cols, mu, 0, i, j, lo, hi) * values[j] + link(cols, mu, 1, i, j, lo, hi) * spun[j]
            total = term if total is None else total + term
        out.append(total)
    return out


def kernel_prepare(odd_ref, v_hbm, g_hbm, vt_ref, za_ref, zb_ref, xa_ref, xb_ref, cols_ref, v_ref, g_ref, sem):
    copy_g = pltpu.make_async_copy(g_hbm, g_ref, sem.at[0])
    copy_v = pltpu.make_async_copy(v_hbm, v_ref, sem.at[1])
    copy_g.start()
    copy_v.start()
    copy_g.wait()
    cols = g_ref[:, 0, :].T
    cols_ref[...] = cols
    copy_v.wait()
    values = []
    for c in range(3):
        both = jnp.concatenate([v_ref[c * 64 : (c + 1) * 64, 0, :], v_ref[192 + c * 64 : 256 + c * 64, 0, :]], axis=0)
        values.append(both.T)
    back = carry(cols, 2, values, True, 0, SITES)
    edge = carry(cols, 1, [v[SITES - ROW :] for v in values], True, SITES - ROW, SITES)
    plane_odd = odd_ref[0] == 1
    block_odd = odd_ref[1] == 1
    for c in range(3):
        vt_ref[c] = values[c]
        za_ref[c] = jnp.where(plane_odd, values[c], back[c])
        zb_ref[c] = jnp.where(plane_odd, back[c], values[c])
        xa_ref[c] = jnp.where(block_odd, values[c][:ROW], edge[c])
        xb_ref[c] = jnp.where(block_odd, edge[c], values[c][:ROW])


def kernel_inner(vt_ref, cols_ref, acc_ref):
    cols = cols_ref[...]
    values = [vt_ref[c] for c in range(3)]
    x_coord = lax.broadcasted_iota(jnp.int32, (SITES, 128), 0) % LX
    ahead = [jnp.where(x_coord == LX - 1, roll(v, LX - 1, 0), roll(v, -1, 0)) for v in values]
    fwd = carry(cols, 0, ahead, False, 0, SITES)
    back = carry(cols, 0, values, True, 0, SITES)
    back = [jnp.where(x_coord == 0, roll(b, -(LX - 1), 0), roll(b, 1, 0)) for b in back]
    up = carry(cols, 1, [v[ROW:] for v in values], False, 0, SITES - ROW)
    down = carry(cols, 1, [v[: SITES - ROW] for v in values], True, 0, SITES - ROW)
    zero = jnp.zeros((ROW, 128), F32)
    for c in range(3):
        inner_y = jnp.concatenate([up[c], zero], axis=0) + jnp.concatenate([zero, down[c]], axis=0)
        acc_ref[c] = (1.0 - 6.0 * KAPPA) * values[c] + KAPPA * (fwd[c] + back[c]) + KAPPA * inner_y


def kernel_smear(odd_ref, acc_ref, cols_ref, za_ref, zb_ref, xa_ref, xb_ref, send_ref):
    cols = cols_ref[...]
    plane_odd = odd_ref[0] == 1
    block_odd = odd_ref[1] == 1
    fwd = carry(cols, 2, [jnp.where(plane_odd, zb_ref[c], za_ref[c]) for c in range(3)], False, 0, SITES)
    edge = carry(cols, 1, [jnp.where(block_odd, xb_ref[c], xa_ref[c]) for c in range(3)], False, SITES - ROW, SITES)
    middle = jnp.zeros((SITES - 2 * ROW, 128), F32)
    for c in range(3):
        below = jnp.where(plane_odd, za_ref[c], zb_ref[c])
        row_below = jnp.where(block_odd, xa_ref[c], xb_ref[c])
        rims = jnp.concatenate([row_below, middle, edge[c]], axis=0)
        total = acc_ref[c] + KAPPA * rims + KAPPA * (fwd[c] + below)
        rounded = total.astype(BF16)
        for k in range(4):
            send_ref[k, c] = rounded


def kernel_output(s_ref, out_ref):
    for c in range(3):
        flat = s_ref[0, c].astype(F32).T
        out_ref[0, c] = flat[:64].astype(BF16)
        out_ref[1, c] = flat[64:].astype(BF16)


def kernel_contract(s_ref, ph_ref, out_ref, wide_ref, spun_ref, lhs_ref, rhs_ref, wave_ref, *, scale):
    phase = ph_ref[...]
    high = phase.astype(BF16)
    rest = phase - high.astype(F32)
    middle = rest.astype(BF16)
    low = (rest - middle.astype(F32)).astype(BF16)
    split = jnp.concatenate([high.astype(F32), middle.astype(F32), low.astype(F32)], axis=0).T.astype(BF16)
    row = lax.broadcasted_iota(jnp.int32, (48, 256), 0) % 16
    lane = lax.broadcasted_iota(jnp.int32, (48, 256), 1) // 128

    def spread_phase(p):
        ones = jnp.where(row == p + 8 * lane, 1.0, 0.0).astype(BF16)
        wave_ref[p] = jnp.dot(split, ones, preferred_element_type=F32)

    spread_phase(0)
    for k in range(4):
        for c in range(3):
            at = (k * 3 + c) * SITES
            wide = s_ref[k, c].astype(F32)
            wide_ref[at : at + SITES] = wide
            spun_ref[at : at + SITES] = turned(wide)
            lhs_ref[:, at : at + SITES] = wide.T.astype(BF16)
    sign = half_sign((64, 128), 1.0)
    for pair in range(4):
        for pp in range(2):
            p = pair * 2 + pp
            if p < 7:
                spread_phase(p + 1)
            for k in range(4):
                for r in range(0, SITES, 16):
                    site = k * SITES + r
                    cos = wave_ref[p, site : site + 16, :128]
                    sin = wave_ref[p, site : site + 16, 128:]
                    for c in range(3):
                        at = (k * 3 + c) * SITES + r
                        value = wide_ref[at : at + 16] * cos + spun_ref[at : at + 16] * sin
                        rhs_ref[pair, at : at + 16, pp * 128 : (pp + 1) * 128] = value.astype(BF16)
        prod = jnp.dot(lhs_ref[...], rhs_ref[pair], preferred_element_type=F32)
        for pp in range(2):
            block = prod[:, pp * 128 : (pp + 1) * 128]
            result = (block[:64] + roll(block[64:], 64, 1) * sign) * scale
            z_at = pp * 2 + pair // 2
            out_ref[z_at, pair % 2] = result[:32]
            out_ref[z_at, 2 + pair % 2] = result[32:]


def kernel_factors(p_ref, out_ref):
    for t0 in range(4):
        for q in range(16):
            real = p_ref[t0, 0, q].astype(F32)
            imag = p_ref[t0, 1, q].astype(F32)
            at = q * 128
            out_ref[t0, :64, at : at + 128] = jnp.concatenate([real, imag], axis=1).astype(BF16)
            out_ref[t0, 64:, at : at + 128] = jnp.concatenate([-imag, real], axis=1).astype(BF16)


def kernel_correlate(tm_ref, e_ref, b_ref, out_ref):
    own = tm_ref[0]
    flip = []
    for pp in range(2):
        phi = jnp.concatenate([e_ref[2 * pp, own], e_ref[2 * pp + 1, own]], axis=0)
        for k in range(16):
            out_ref[k, pp * 64 : (pp + 1) * 64] = phi
        tall = phi.astype(F32).T
        flip.append(jnp.concatenate([tall[:64], tall[64:]], axis=1))
    sign = half_sign((64, 128), 1.0)
    row = lax.broadcasted_iota(jnp.int32, (16, 128), 0)
    lane = lax.broadcasted_iota(jnp.int32, (16, 128), 1)
    tile = jnp.zeros((16, 128), F32)
    for t0 in range(4):
        weights = []
        for pp in range(2):
            far = jnp.concatenate([e_ref[2 * pp, t0], e_ref[2 * pp + 1, t0]], axis=0)
            weights.append(far)
            weights.append(turned(far.astype(F32)).astype(BF16))
        weights = jnp.concatenate(weights, axis=0)
        first = jnp.concatenate([b_ref[t0, :64, q * 128 : (q + 1) * 128] for q in range(16)], axis=0)
        left = lax.dot_general(first, weights, NT_DIMS, preferred_element_type=F32).astype(BF16)
        tall = []
        for pp in range(2):
            tall.append(
                jnp.concatenate([left[q * 64 : (q + 1) * 64, pp * 128 : (pp + 1) * 128] for q in range(16)], axis=1)
            )
        tall = jnp.concatenate(tall, axis=0)
        right = lax.dot_general(tall, b_ref[t0], NT_DIMS, preferred_element_type=F32)
        for pp in range(2):
            block = right[pp * 64 : (pp + 1) * 64]
            real = jnp.sum(flip[pp] * block * sign) * (1.0 / NEV)
            imag = jnp.sum(flip[pp] * roll(block, 64, 1)) * (1.0 / NEV)
            tile = jnp.where((row == pp) & (lane % 8 == t0), real, tile)
            tile = jnp.where((row == pp) & (lane % 8 == 4 + t0), imag, tile)
    high = tile.astype(BF16).astype(F32)
    middle = (tile - high).astype(BF16).astype(F32)
    low = tile - high - middle
    packed = jnp.where(lane < 8, high, jnp.where(lane < 16, middle, low)).astype(BF16)
    for k in range(16):
        out_ref[k, 128:144] = packed


def kernel_unpack(r_ref, e_ref, c_ref):
    rows = jnp.concatenate([r_ref[s, 128:144].astype(F32)[:2] for s in range(16)], axis=0)
    total = (rows + roll(rows, -8, 1)) + roll(rows, -16, 1)
    tall = total.T
    c_ref[0] = tall[:4]
    c_ref[1] = tall[4:8]
    for s in range(16):
        for pp in range(2):
            both = r_ref[s, pp * 64 : (pp + 1) * 64]
            e_ref[2 * s + pp, 0] = both[:, :64]
            e_ref[2 * s + pp, 1] = both[:, 64:]


def shape(dims, dtype):
    return jax.ShapeDtypeStruct(dims, dtype)


def run(kernel, outs, args, scratch=(), scalar=False, raw=False):
    in_specs = None
    if raw:
        in_specs = [pl.BlockSpec(memory_space=pltpu.SMEM)] + [pl.BlockSpec(memory_space=pltpu.HBM)] * (len(args) - 1)
    elif scalar:
        in_specs = [pl.BlockSpec(memory_space=pltpu.SMEM)] + [pl.BlockSpec(memory_space=pltpu.VMEM)] * (len(args) - 1)
    else:
        in_specs = [pl.BlockSpec(memory_space=pltpu.VMEM)] * len(args)
    return pl.pallas_call(
        kernel,
        out_shape=outs,
        in_specs=in_specs,
        out_specs=jax.tree.map(lambda _: pl.BlockSpec(memory_space=pltpu.VMEM), outs),
        scratch_shapes=list(scratch),
        compiler_params=pltpu.CompilerParams(vmem_limit_bytes=48 << 20),
    )(*args)


def phases(momenta, z_index):
    site = jnp.arange(4 * SITES, dtype=jnp.int32)
    turn_x = momenta[:, 0, None] * (site % LX)[None] % LX
    turn_y = momenta[:, 1, None] * (site // LX)[None] % LX
    turn_z = momenta[:, 2, None] * z_index % NZ
    angles = (
        2.0
        * math.pi
        * (turn_x.astype(F32) / LX + turn_y.astype(F32) / LX + turn_z.astype(F32) / NZ)
    )
    return jnp.concatenate([jnp.cos(angles), -jnp.sin(angles)], axis=0)


def swap(value, axes):
    return lax.all_to_all(value, axes, split_axis=0, concat_axis=0, tiled=True)


def spread(value, axes, count):
    return swap(jnp.broadcast_to(value[None], (count,) + value.shape), axes)


def local(eigvecs, gauge_links, perambulators, momenta):
    planes = ("zh", "zu", "zd", "yu", "yd")
    pairs_a = [(i, i ^ 1) for i in range(NZ)]
    pairs_b = [(i, ((i + 1) ^ 1) - 1) for i in range(NZ)]
    pairs_b = [(i, j % NZ) for i, j in pairs_b]
    ring_a = [(i, i ^ 1) for i in range(4)]
    ring_b = [(i, (((i + 1) ^ 1) - 1) % 4) for i in range(4)]
    z_index = lax.axis_index(planes)
    x_index = lax.axis_index("x")
    tm_index = lax.axis_index(("yh", "c"))
    odd = jnp.stack([lax.axis_index("yd"), x_index % 2]).astype(jnp.int32)

    field = eigvecs.reshape(6 * NEV, 1, SITES)
    links = gauge_links.reshape(54, 1, SITES)
    site_shape = shape((3, SITES, 128), F32)
    row_shape = shape((3, ROW, 128), F32)
    values, send_za, send_zb, send_xa, send_xb, cols = run(
        kernel_prepare,
        (site_shape, site_shape, site_shape, row_shape, row_shape, shape((SITES, 54), F32)),
        (
            odd,
            pltpu.with_memory_space_constraint(field, pltpu.HBM),
            pltpu.with_memory_space_constraint(links, pltpu.HBM),
        ),
        scratch=[
            pltpu.VMEM((6 * NEV, 1, SITES), F32),
            pltpu.VMEM((54, 1, SITES), F32),
            pltpu.SemaphoreType.DMA((2,)),
        ],
        raw=True,
    )
    recv_za = lax.ppermute(send_za, planes, pairs_a)
    recv_zb = lax.ppermute(send_zb, planes, pairs_b)
    recv_xa = lax.ppermute(send_xa, "x", ring_a)
    recv_xb = lax.ppermute(send_xb, "x", ring_b)

    inner = run(kernel_inner, site_shape, (values, cols))
    send = run(
        kernel_smear,
        shape((4, 3, SITES, 128), BF16),
        (odd, inner, cols, recv_za, recv_zb, recv_xa, recv_xb),
        scalar=True,
    )
    mine = lax.dynamic_index_in_dim(momenta.reshape(4, 4, 2, 3), x_index, 1, keepdims=False).reshape(8, 3)
    phase = phases(mine, z_index)
    send, phase = lax.optimization_barrier((send, phase))
    shared = swap(send, "x")
    scale = 1.0 / math.sqrt(3.0 * NZ * LX * LX)

    def contract(*refs):
        kernel_contract(*refs, scale=scale)

    partial = run(
        contract,
        shape((4, 4, 32, 128), F32),
        (shared, phase),
        scratch=[
            pltpu.VMEM((12 * SITES, 128), F32),
            pltpu.VMEM((12 * SITES, 128), F32),
            pltpu.VMEM((128, 12 * SITES), BF16),
            pltpu.VMEM((4, 12 * SITES, 256), BF16),
            pltpu.VMEM((8, 4 * SITES, 256), F32),
        ],
    )
    pieces = swap(partial.reshape(16, 32, 128), ("zu", "zd", "yu", "yd"))
    part = jnp.sum(pieces, axis=0)
    part = jnp.sum(spread(part, "zh", 3), axis=0)
    part, perambulators, send = lax.optimization_barrier((part.astype(BF16), perambulators, send))
    near = spread(part, ("zu", "yu", "yh", "c"), 16).reshape(4, 4, 32, 128)
    factors = run(kernel_factors, shape((4, 128, 16 * 128), BF16), (perambulators.reshape(4, 2, 16, NEV, NEV),))

    smeared = run(kernel_output, shape((2, 3, NEV, SITES), BF16), (send,))
    payload = run(
        kernel_correlate,
        shape((16, 144, 128), BF16),
        (tm_index.astype(jnp.int32).reshape(1), near, factors),
        scalar=True,
    )
    payload, smeared = lax.optimization_barrier((payload, smeared))
    everything = swap(payload, ("zd", "yd", "x"))
    elementals, correlator = run(kernel_unpack, (shape((32, 2, NEV, NEV), BF16), shape((2, 4, 32), F32)), (everything,))
    return (
        smeared.reshape(1, 2, 3, NEV, 1, SITES),
        elementals.reshape(32, 1, 2, NEV, NEV),
        jnp.swapaxes(correlator, 1, 2).reshape(2, 32, 1, 4),
    )


def solution(mesh):
    fine = Mesh(mesh.devices.reshape(3, 2, 2, 2, 2, 4, 2, 2), ("zh", "zu", "zd", "yu", "yd", "x", "yh", "c"))
    space = ("zh", "zu", "zd", "yu", "yd", "x")
    times = ("yh", "c")

    return jax.shard_map(
        local,
        mesh=fine,
        in_specs=(
            P(times, None, None, None, space, None),
            P(None, times, None, None, None, space, None),
            P(times, None, None, None, None, None, None),
            P(),
        ),
        out_specs=(
            P(times, None, None, None, space, None),
            P(None, times, None, None, None),
            P(None, None, times, None),
        ),
        check_vma=False,
    )
```

```python
import math

import jax
import jax.numpy as jnp
from jax import lax
from jax.experimental import pallas as pl
from jax.experimental.pallas import tpu as pltpu
from jax.sharding import Mesh, PartitionSpec as P


NEV = 64
LX = 24
NZ = 48
SITES = 144
ROW = LX
KAPPA = 0.25
F32 = jnp.float32
BF16 = jnp.bfloat16
NT_DIMS = (((1,), (1,)), ((), ()))

USE_PALLAS = True


def roll(x, shift, axis):
    shift = shift % x.shape[axis]
    if USE_PALLAS:
        return pltpu.roll(x, shift, axis)
    return jnp.roll(x, shift, axis)


def half_sign(shape, low):
    lane = lax.broadcasted_iota(jnp.int32, shape, len(shape) - 1)
    return jnp.where(lane < 64, low, -low).astype(F32)


def turned(x):
    return roll(x, 64, 1) * half_sign(x.shape, -1.0)


def link(cols, mu, part, row, col, lo, hi):
    index = ((mu * 2 + part) * 3 + row) * 3 + col
    return cols[lo:hi, index : index + 1]


def carry(cols, mu, values, adjoint, lo, hi):
    spun = [turned(v) for v in values]
    out = []
    for i in range(3):
        total = None
        for j in range(3):
            if adjoint:
                term = link(cols, mu, 0, j, i, lo, hi) * values[j] - link(cols, mu, 1, j, i, lo, hi) * spun[j]
            else:
                term = link(cols, mu, 0, i, j, lo, hi) * values[j] + link(cols, mu, 1, i, j, lo, hi) * spun[j]
            total = term if total is None else total + term
        out.append(total)
    return out


def kernel_prepare(odd_ref, v_hbm, g_hbm, vt_ref, za_ref, zb_ref, xa_ref, xb_ref, cols_ref, v_ref, g_ref, sem):
    copy_g = pltpu.make_async_copy(g_hbm, g_ref, sem.at[0])
    copy_v = pltpu.make_async_copy(v_hbm, v_ref, sem.at[1])
    copy_g.start()
    copy_v.start()
    copy_g.wait()
    cols = g_ref[:, 0, :].T
    cols_ref[...] = cols
    copy_v.wait()
    values = []
    for c in range(3):
        both = jnp.concatenate([v_ref[c * 64 : (c + 1) * 64, 0, :], v_ref[192 + c * 64 : 256 + c * 64, 0, :]], axis=0)
        values.append(both.T)
    back = carry(cols, 2, values, True, 0, SITES)
    edge = carry(cols, 1, [v[SITES - ROW :] for v in values], True, SITES - ROW, SITES)
    plane_odd = odd_ref[0] == 1
    block_odd = odd_ref[1] == 1
    for c in range(3):
        vt_ref[c] = values[c]
        za_ref[c] = jnp.where(plane_odd, values[c], back[c])
        zb_ref[c] = jnp.where(plane_odd, back[c], values[c])
        xa_ref[c] = jnp.where(block_odd, values[c][:ROW], edge[c])
        xb_ref[c] = jnp.where(block_odd, edge[c], values[c][:ROW])


def kernel_inner(vt_ref, cols_ref, acc_ref):
    cols = cols_ref[...]
    values = [vt_ref[c] for c in range(3)]
    x_coord = lax.broadcasted_iota(jnp.int32, (SITES, 128), 0) % LX
    ahead = [jnp.where(x_coord == LX - 1, roll(v, LX - 1, 0), roll(v, -1, 0)) for v in values]
    fwd = carry(cols, 0, ahead, False, 0, SITES)
    back = carry(cols, 0, values, True, 0, SITES)
    back = [jnp.where(x_coord == 0, roll(b, -(LX - 1), 0), roll(b, 1, 0)) for b in back]
    up = carry(cols, 1, [v[ROW:] for v in values], False, 0, SITES - ROW)
    down = carry(cols, 1, [v[: SITES - ROW] for v in values], True, 0, SITES - ROW)
    zero = jnp.zeros((ROW, 128), F32)
    for c in range(3):
        inner_y = jnp.concatenate([up[c], zero], axis=0) + jnp.concatenate([zero, down[c]], axis=0)
        acc_ref[c] = (1.0 - 6.0 * KAPPA) * values[c] + KAPPA * (fwd[c] + back[c]) + KAPPA * inner_y


def kernel_smear(odd_ref, acc_ref, cols_ref, za_ref, zb_ref, xa_ref, xb_ref, send_ref):
    cols = cols_ref[...]
    plane_odd = odd_ref[0] == 1
    block_odd = odd_ref[1] == 1
    fwd = carry(cols, 2, [jnp.where(plane_odd, zb_ref[c], za_ref[c]) for c in range(3)], False, 0, SITES)
    edge = carry(cols, 1, [jnp.where(block_odd, xb_ref[c], xa_ref[c]) for c in range(3)], False, SITES - ROW, SITES)
    middle = jnp.zeros((SITES - 2 * ROW, 128), F32)
    for c in range(3):
        below = jnp.where(plane_odd, za_ref[c], zb_ref[c])
        row_below = jnp.where(block_odd, xa_ref[c], xb_ref[c])
        rims = jnp.concatenate([row_below, middle, edge[c]], axis=0)
        total = acc_ref[c] + KAPPA * rims + KAPPA * (fwd[c] + below)
        rounded = total.astype(BF16)
        for k in range(4):
            send_ref[k, c] = rounded


def kernel_output(s_ref, out_ref):
    for c in range(3):
        flat = s_ref[0, c].astype(F32).T
        out_ref[0, c] = flat[:64].astype(BF16)
        out_ref[1, c] = flat[64:].astype(BF16)


def kernel_contract(s_ref, ph_ref, out_ref, wide_ref, spun_ref, lhs_ref, rhs_ref, wave_ref, *, scale):
    phase = ph_ref[...]
    high = phase.astype(BF16)
    rest = phase - high.astype(F32)
    middle = rest.astype(BF16)
    low = (rest - middle.astype(F32)).astype(BF16)
    split = jnp.concatenate([high.astype(F32), middle.astype(F32), low.astype(F32)], axis=0).T.astype(BF16)
    row = lax.broadcasted_iota(jnp.int32, (48, 256), 0) % 16
    lane = lax.broadcasted_iota(jnp.int32, (48, 256), 1) // 128

    def spread_phase(p):
        ones = jnp.where(row == p + 8 * lane, 1.0, 0.0).astype(BF16)
        wave_ref[p] = jnp.dot(split, ones, preferred_element_type=F32)

    spread_phase(0)
    for k in range(4):
        for c in range(3):
            at = (k * 3 + c) * SITES
            wide = s_ref[k, c].astype(F32)
            wide_ref[at : at + SITES] = wide
            spun_ref[at : at + SITES] = turned(wide)
            lhs_ref[:, at : at + SITES] = wide.T.astype(BF16)
    sign = half_sign((64, 128), 1.0)
    for pair in range(4):
        for pp in range(2):
            p = pair * 2 + pp
            if p < 7:
                spread_phase(p + 1)
            for k in range(4):
                for r in range(0, SITES, 16):
                    site = k * SITES + r
                    cos = wave_ref[p, site : site + 16, :128]
                    sin = wave_ref[p, site : site + 16, 128:]
                    for c in range(3):
                        at = (k * 3 + c) * SITES + r
                        value = wide_ref[at : at + 16] * cos + spun_ref[at : at + 16] * sin
                        rhs_ref[pair, at : at + 16, pp * 128 : (pp + 1) * 128] = value.astype(BF16)
        prod = jnp.dot(lhs_ref[...], rhs_ref[pair], preferred_element_type=F32)
        for pp in range(2):
            block = prod[:, pp * 128 : (pp + 1) * 128]
            result = (block[:64] + roll(block[64:], 64, 1) * sign) * scale
            out_ref[pp * 2, pair] = result[:32]
            out_ref[pp * 2 + 1, pair] = result[32:]


def kernel_factors(p_ref, out_ref):
    for t0 in range(4):
        for q in range(16):
            real = p_ref[t0, 0, q].astype(F32)
            imag = p_ref[t0, 1, q].astype(F32)
            at = q * 128
            out_ref[t0, :64, at : at + 128] = jnp.concatenate([real, imag], axis=1).astype(BF16)
            out_ref[t0, 64:, at : at + 128] = jnp.concatenate([-imag, real], axis=1).astype(BF16)


def kernel_correlate(tm_ref, e_ref, b_ref, out_ref):
    own = tm_ref[0]
    flip = []
    for pp in range(2):
        phi = jnp.concatenate([e_ref[2 * pp, own], e_ref[2 * pp + 1, own]], axis=0)
        for k in range(16):
            out_ref[k, pp * 64 : (pp + 1) * 64] = phi
        tall = phi.astype(F32).T
        flip.append(jnp.concatenate([tall[:64], tall[64:]], axis=1))
    sign = half_sign((64, 128), 1.0)
    row = lax.broadcasted_iota(jnp.int32, (16, 128), 0)
    lane = lax.broadcasted_iota(jnp.int32, (16, 128), 1)
    tile = jnp.zeros((16, 128), F32)
    for t0 in range(4):
        weights = []
        for pp in range(2):
            far = jnp.concatenate([e_ref[2 * pp, t0], e_ref[2 * pp + 1, t0]], axis=0)
            weights.append(far)
            weights.append(turned(far.astype(F32)).astype(BF16))
        weights = jnp.concatenate(weights, axis=0)
        first = jnp.concatenate([b_ref[t0, :64, q * 128 : (q + 1) * 128] for q in range(16)], axis=0)
        left = lax.dot_general(first, weights, NT_DIMS, preferred_element_type=F32).astype(BF16)
        tall = []
        for pp in range(2):
            tall.append(
                jnp.concatenate([left[q * 64 : (q + 1) * 64, pp * 128 : (pp + 1) * 128] for q in range(16)], axis=1)
            )
        tall = jnp.concatenate(tall, axis=0)
        right = lax.dot_general(tall, b_ref[t0], NT_DIMS, preferred_element_type=F32)
        for pp in range(2):
            block = right[pp * 64 : (pp + 1) * 64]
            real = jnp.sum(flip[pp] * block * sign) * (1.0 / NEV)
            imag = jnp.sum(flip[pp] * roll(block, 64, 1)) * (1.0 / NEV)
            tile = jnp.where((row == pp) & (lane % 8 == t0), real, tile)
            tile = jnp.where((row == pp) & (lane % 8 == 4 + t0), imag, tile)
    high = tile.astype(BF16).astype(F32)
    middle = (tile - high).astype(BF16).astype(F32)
    low = tile - high - middle
    packed = jnp.where(lane < 8, high, jnp.where(lane < 16, middle, low)).astype(BF16)
    for k in range(16):
        out_ref[k, 128:144] = packed


def kernel_unpack(r_ref, e_ref, c_ref):
    rows = jnp.concatenate([r_ref[s, 128:144].astype(F32)[:2] for s in range(16)], axis=0)
    total = (rows + roll(rows, -8, 1)) + roll(rows, -16, 1)
    tall = total.T
    c_ref[0] = tall[:4]
    c_ref[1] = tall[4:8]
    for s in range(16):
        for pp in range(2):
            both = r_ref[s, pp * 64 : (pp + 1) * 64]
            e_ref[2 * s + pp, 0] = both[:, :64]
            e_ref[2 * s + pp, 1] = both[:, 64:]


def shape(dims, dtype):
    return jax.ShapeDtypeStruct(dims, dtype)


def run(kernel, outs, args, scratch=(), scalar=False, raw=False):
    in_specs = None
    if raw:
        in_specs = [pl.BlockSpec(memory_space=pltpu.SMEM)] + [pl.BlockSpec(memory_space=pltpu.HBM)] * (len(args) - 1)
    elif scalar:
        in_specs = [pl.BlockSpec(memory_space=pltpu.SMEM)] + [pl.BlockSpec(memory_space=pltpu.VMEM)] * (len(args) - 1)
    else:
        in_specs = [pl.BlockSpec(memory_space=pltpu.VMEM)] * len(args)
    return pl.pallas_call(
        kernel,
        out_shape=outs,
        in_specs=in_specs,
        out_specs=jax.tree.map(lambda _: pl.BlockSpec(memory_space=pltpu.VMEM), outs),
        scratch_shapes=list(scratch),
        compiler_params=pltpu.CompilerParams(vmem_limit_bytes=48 << 20),
    )(*args)


def phases(momenta, z_base, y_base):
    site = jnp.arange(4 * SITES, dtype=jnp.int32)
    block = site // SITES
    row = site % SITES // LX
    turn_x = momenta[:, 0, None] * (site % LX)[None] % LX
    turn_y = momenta[:, 1, None] * (y_base + row)[None] % LX
    turn_z = momenta[:, 2, None] * (z_base + block // 2 * 4 + block % 2)[None] % NZ
    angles = (
        2.0
        * math.pi
        * (turn_x.astype(F32) / LX + turn_y.astype(F32) / LX + turn_z.astype(F32) / NZ)
    )
    return jnp.concatenate([jnp.cos(angles), -jnp.sin(angles)], axis=0)


def swap(value, axes):
    return lax.all_to_all(value, axes, split_axis=0, concat_axis=0, tiled=True)


def spread(value, axes, count):
    return swap(jnp.broadcast_to(value[None], (count,) + value.shape), axes)


def local(eigvecs, gauge_links, perambulators, momenta):
    planes = ("zh", "zu", "zd", "yu", "yd")
    pairs_a = [(i, i ^ 1) for i in range(NZ)]
    pairs_b = [(i, ((i + 1) ^ 1) - 1) for i in range(NZ)]
    pairs_b = [(i, j % NZ) for i, j in pairs_b]
    ring_a = [(i, i ^ 1) for i in range(4)]
    ring_b = [(i, (((i + 1) ^ 1) - 1) % 4) for i in range(4)]
    octet = lax.axis_index(("zd", "yd"))
    z_base = lax.axis_index("zh") * 16 + lax.axis_index("zu") * 8 + lax.axis_index("yu") * 2
    x_index = lax.axis_index("x")
    tm_index = lax.axis_index(("yh", "c"))
    odd = jnp.stack([lax.axis_index("yd"), x_index % 2]).astype(jnp.int32)

    field = eigvecs.reshape(6 * NEV, 1, SITES)
    links = gauge_links.reshape(54, 1, SITES)
    site_shape = shape((3, SITES, 128), F32)
    row_shape = shape((3, ROW, 128), F32)
    values, send_za, send_zb, send_xa, send_xb, cols = run(
        kernel_prepare,
        (site_shape, site_shape, site_shape, row_shape, row_shape, shape((SITES, 54), F32)),
        (
            odd,
            pltpu.with_memory_space_constraint(field, pltpu.HBM),
            pltpu.with_memory_space_constraint(links, pltpu.HBM),
        ),
        scratch=[
            pltpu.VMEM((6 * NEV, 1, SITES), F32),
            pltpu.VMEM((54, 1, SITES), F32),
            pltpu.SemaphoreType.DMA((2,)),
        ],
        raw=True,
    )
    recv_za = lax.ppermute(send_za, planes, pairs_a)
    recv_zb = lax.ppermute(send_zb, planes, pairs_b)
    recv_xa = lax.ppermute(send_xa, "x", ring_a)
    recv_xb = lax.ppermute(send_xb, "x", ring_b)

    inner = run(kernel_inner, site_shape, (values, cols))
    send = run(
        kernel_smear,
        shape((4, 3, SITES, 128), BF16),
        (odd, inner, cols, recv_za, recv_zb, recv_xa, recv_xb),
        scalar=True,
    )
    mine = lax.dynamic_index_in_dim(momenta.reshape(4, 8, 3), octet, 0, keepdims=False)
    phase = phases(mine, z_base, x_index * (SITES // LX))
    send, phase = lax.optimization_barrier((send, phase))
    shared = swap(send, ("zd", "yd"))
    scale = 1.0 / math.sqrt(3.0 * NZ * LX * LX)

    def contract(*refs):
        kernel_contract(*refs, scale=scale)

    partial = run(
        contract,
        shape((4, 4, 32, 128), F32),
        (shared, phase),
        scratch=[
            pltpu.VMEM((12 * SITES, 128), F32),
            pltpu.VMEM((12 * SITES, 128), F32),
            pltpu.VMEM((128, 12 * SITES), BF16),
            pltpu.VMEM((4, 12 * SITES, 256), BF16),
            pltpu.VMEM((8, 4 * SITES, 256), F32),
        ],
    )
    pieces = swap(partial.reshape(16, 32, 128), ("zu", "yu", "x"))
    part = jnp.sum(pieces, axis=0)
    part = jnp.sum(spread(part, "zh", 3), axis=0)
    part, perambulators, send = lax.optimization_barrier((part.astype(BF16), perambulators, send))
    near = spread(part, ("zu", "yu", "yh", "c"), 16).reshape(4, 4, 32, 128)
    factors = run(kernel_factors, shape((4, 128, 16 * 128), BF16), (perambulators.reshape(4, 2, 16, NEV, NEV),))

    smeared = run(kernel_output, shape((2, 3, NEV, SITES), BF16), (send,))
    payload = run(
        kernel_correlate,
        shape((16, 144, 128), BF16),
        (tm_index.astype(jnp.int32).reshape(1), near, factors),
        scalar=True,
    )
    payload, smeared = lax.optimization_barrier((payload, smeared))
    everything = swap(payload, ("zd", "yd", "x"))
    elementals, correlator = run(kernel_unpack, (shape((32, 2, NEV, NEV), BF16), shape((2, 4, 32), F32)), (everything,))
    return (
        smeared.reshape(1, 2, 3, NEV, 1, SITES),
        elementals.reshape(32, 1, 2, NEV, NEV),
        jnp.swapaxes(correlator, 1, 2).reshape(2, 32, 1, 4),
    )


def solution(mesh):
    fine = Mesh(mesh.devices.reshape(3, 2, 2, 2, 2, 4, 2, 2), ("zh", "zu", "zd", "yu", "yd", "x", "yh", "c"))
    space = ("zh", "zu", "zd", "yu", "yd", "x")
    times = ("yh", "c")

    return jax.shard_map(
        local,
        mesh=fine,
        in_specs=(
            P(times, None, None, None, space, None),
            P(None, times, None, None, None, space, None),
            P(times, None, None, None, None, None, None),
            P(),
        ),
        out_specs=(
            P(times, None, None, None, space, None),
            P(None, times, None, None, None),
            P(None, None, times, None),
        ),
        check_vma=False,
    )
```

```python
import math

import jax
import jax.numpy as jnp
from jax import lax
from jax.experimental import pallas as pl
from jax.experimental.pallas import tpu as pltpu
from jax.sharding import Mesh, PartitionSpec as P


NEV = 64
LX = 24
NZ = 48
SITES = 144
ROW = LX
KAPPA = 0.25
F32 = jnp.float32
BF16 = jnp.bfloat16
NT_DIMS = (((1,), (1,)), ((), ()))

USE_PALLAS = True


def roll(x, shift, axis):
    shift = shift % x.shape[axis]
    if USE_PALLAS:
        return pltpu.roll(x, shift, axis)
    return jnp.roll(x, shift, axis)


def half_sign(shape, low):
    lane = lax.broadcasted_iota(jnp.int32, shape, len(shape) - 1)
    return jnp.where(lane < 64, low, -low).astype(F32)


def turned(x):
    return roll(x, 64, 1) * half_sign(x.shape, -1.0)


def link(cols, mu, part, row, col, lo, hi):
    index = ((mu * 2 + part) * 3 + row) * 3 + col
    return cols[lo:hi, index : index + 1]


def carry(cols, mu, values, adjoint, lo, hi):
    spun = [turned(v) for v in values]
    out = []
    for i in range(3):
        total = None
        for j in range(3):
            if adjoint:
                term = link(cols, mu, 0, j, i, lo, hi) * values[j] - link(cols, mu, 1, j, i, lo, hi) * spun[j]
            else:
                term = link(cols, mu, 0, i, j, lo, hi) * values[j] + link(cols, mu, 1, i, j, lo, hi) * spun[j]
            total = term if total is None else total + term
        out.append(total)
    return out


def kernel_prepare(odd_ref, v_hbm, g_hbm, vt_ref, za_ref, zb_ref, xa_ref, xb_ref, cols_ref, v_ref, g_ref, sem):
    copy_g = pltpu.make_async_copy(g_hbm, g_ref, sem.at[0])
    copy_v = pltpu.make_async_copy(v_hbm, v_ref, sem.at[1])
    copy_g.start()
    copy_v.start()
    copy_g.wait()
    cols = g_ref[:, 0, :].T
    cols_ref[...] = cols
    copy_v.wait()
    values = []
    for c in range(3):
        both = jnp.concatenate([v_ref[c * 64 : (c + 1) * 64, 0, :], v_ref[192 + c * 64 : 256 + c * 64, 0, :]], axis=0)
        values.append(both.T)
    back = carry(cols, 2, values, True, 0, SITES)
    edge = carry(cols, 1, [v[SITES - ROW :] for v in values], True, SITES - ROW, SITES)
    plane_odd = odd_ref[0] == 1
    block_odd = odd_ref[1] == 1
    for c in range(3):
        vt_ref[c] = values[c]
        za_ref[c] = jnp.where(plane_odd, values[c], back[c])
        zb_ref[c] = jnp.where(plane_odd, back[c], values[c])
        xa_ref[c] = jnp.where(block_odd, values[c][:ROW], edge[c])
        xb_ref[c] = jnp.where(block_odd, edge[c], values[c][:ROW])


def kernel_inner(vt_ref, cols_ref, acc_ref):
    cols = cols_ref[...]
    values = [vt_ref[c] for c in range(3)]
    x_coord = lax.broadcasted_iota(jnp.int32, (SITES, 128), 0) % LX
    ahead = [jnp.where(x_coord == LX - 1, roll(v, LX - 1, 0), roll(v, -1, 0)) for v in values]
    fwd = carry(cols, 0, ahead, False, 0, SITES)
    back = carry(cols, 0, values, True, 0, SITES)
    back = [jnp.where(x_coord == 0, roll(b, -(LX - 1), 0), roll(b, 1, 0)) for b in back]
    up = carry(cols, 1, [v[ROW:] for v in values], False, 0, SITES - ROW)
    down = carry(cols, 1, [v[: SITES - ROW] for v in values], True, 0, SITES - ROW)
    zero = jnp.zeros((ROW, 128), F32)
    for c in range(3):
        inner_y = jnp.concatenate([up[c], zero], axis=0) + jnp.concatenate([zero, down[c]], axis=0)
        acc_ref[c] = (1.0 - 6.0 * KAPPA) * values[c] + KAPPA * (fwd[c] + back[c]) + KAPPA * inner_y


def kernel_smear(odd_ref, acc_ref, cols_ref, za_ref, zb_ref, xa_ref, xb_ref, send_ref):
    cols = cols_ref[...]
    plane_odd = odd_ref[0] == 1
    block_odd = odd_ref[1] == 1
    fwd = carry(cols, 2, [jnp.where(plane_odd, zb_ref[c], za_ref[c]) for c in range(3)], False, 0, SITES)
    edge = carry(cols, 1, [jnp.where(block_odd, xb_ref[c], xa_ref[c]) for c in range(3)], False, SITES - ROW, SITES)
    middle = jnp.zeros((SITES - 2 * ROW, 128), F32)
    for c in range(3):
        below = jnp.where(plane_odd, za_ref[c], zb_ref[c])
        row_below = jnp.where(block_odd, xa_ref[c], xb_ref[c])
        rims = jnp.concatenate([row_below, middle, edge[c]], axis=0)
        total = acc_ref[c] + KAPPA * rims + KAPPA * (fwd[c] + below)
        rounded = total.astype(BF16)
        for k in range(4):
            send_ref[k, c] = rounded


def kernel_output(s_ref, out_ref):
    for c in range(3):
        flat = s_ref[0, c].astype(F32).T
        out_ref[0, c] = flat[:64].astype(BF16)
        out_ref[1, c] = flat[64:].astype(BF16)


def kernel_contract(s_ref, ph_ref, out_ref, wide_ref, spun_ref, lhs_ref, rhs_ref, wave_ref, *, scale):
    phase = ph_ref[...]
    high = phase.astype(BF16)
    rest = phase - high.astype(F32)
    middle = rest.astype(BF16)
    low = (rest - middle.astype(F32)).astype(BF16)
    split = jnp.concatenate([high.astype(F32), middle.astype(F32), low.astype(F32)], axis=0).T.astype(BF16)
    row = lax.broadcasted_iota(jnp.int32, (48, 256), 0) % 16
    lane = lax.broadcasted_iota(jnp.int32, (48, 256), 1) // 128

    def spread_phase(p):
        ones = jnp.where(row == p + 8 * lane, 1.0, 0.0).astype(BF16)
        wave_ref[p] = jnp.dot(split, ones, preferred_element_type=F32)

    spread_phase(0)
    for k in range(4):
        for c in range(3):
            at = (k * 3 + c) * SITES
            wide = s_ref[k, c].astype(F32)
            wide_ref[at : at + SITES] = wide
            spun_ref[at : at + SITES] = turned(wide)
            lhs_ref[:, at : at + SITES] = wide.T.astype(BF16)
    sign = half_sign((64, 128), 1.0)
    for pair in range(4):
        for pp in range(2):
            p = pair * 2 + pp
            if p < 7:
                spread_phase(p + 1)
            for k in range(4):
                for r in range(0, SITES, 16):
                    site = k * SITES + r
                    cos = wave_ref[p, site : site + 16, :128]
                    sin = wave_ref[p, site : site + 16, 128:]
                    for c in range(3):
                        at = (k * 3 + c) * SITES + r
                        value = wide_ref[at : at + 16] * cos + spun_ref[at : at + 16] * sin
                        rhs_ref[pair, at : at + 16, pp * 128 : (pp + 1) * 128] = value.astype(BF16)
        prod = jnp.dot(lhs_ref[...], rhs_ref[pair], preferred_element_type=F32)
        for pp in range(2):
            block = prod[:, pp * 128 : (pp + 1) * 128]
            result = (block[:64] + roll(block[64:], 64, 1) * sign) * scale
            z_at = pp * 2 + pair // 2
            out_ref[z_at, pair % 2] = result[:32]
            out_ref[z_at, 2 + pair % 2] = result[32:]


def kernel_factors(p_ref, out_ref):
    for t0 in range(4):
        for q in range(16):
            real = p_ref[t0, 0, q].astype(F32)
            imag = p_ref[t0, 1, q].astype(F32)
            at = q * 128
            out_ref[t0, :64, at : at + 128] = jnp.concatenate([real, imag], axis=1).astype(BF16)
            out_ref[t0, 64:, at : at + 128] = jnp.concatenate([-imag, real], axis=1).astype(BF16)


def kernel_correlate(tm_ref, e_ref, b_ref, out_ref):
    own = tm_ref[0]
    flip = []
    for pp in range(2):
        phi = jnp.concatenate([e_ref[2 * pp, own], e_ref[2 * pp + 1, own]], axis=0)
        for k in range(16):
            out_ref[k, pp * 64 : (pp + 1) * 64] = phi
        tall = phi.astype(F32).T
        flip.append(jnp.concatenate([tall[:64], tall[64:]], axis=1))
    sign = half_sign((64, 128), 1.0)
    row = lax.broadcasted_iota(jnp.int32, (16, 128), 0)
    lane = lax.broadcasted_iota(jnp.int32, (16, 128), 1)
    tile = jnp.zeros((16, 128), F32)
    for t0 in range(4):
        weights = []
        for pp in range(2):
            far = jnp.concatenate([e_ref[2 * pp, t0], e_ref[2 * pp + 1, t0]], axis=0)
            weights.append(far)
            weights.append(turned(far.astype(F32)).astype(BF16))
        weights = jnp.concatenate(weights, axis=0)
        first = jnp.concatenate([b_ref[t0, :64, q * 128 : (q + 1) * 128] for q in range(16)], axis=0)
        left = lax.dot_general(first, weights, NT_DIMS, preferred_element_type=F32).astype(BF16)
        tall = []
        for pp in range(2):
            tall.append(
                jnp.concatenate([left[q * 64 : (q + 1) * 64, pp * 128 : (pp + 1) * 128] for q in range(16)], axis=1)
            )
        tall = jnp.concatenate(tall, axis=0)
        right = lax.dot_general(tall, b_ref[t0], NT_DIMS, preferred_element_type=F32)
        for pp in range(2):
            block = right[pp * 64 : (pp + 1) * 64]
            real = jnp.sum(flip[pp] * block * sign) * (1.0 / NEV)
            imag = jnp.sum(flip[pp] * roll(block, 64, 1)) * (1.0 / NEV)
            tile = jnp.where((row == pp) & (lane % 8 == t0), real, tile)
            tile = jnp.where((row == pp) & (lane % 8 == 4 + t0), imag, tile)
    high = tile.astype(BF16).astype(F32)
    middle = (tile - high).astype(BF16).astype(F32)
    low = tile - high - middle
    packed = jnp.where(lane < 8, high, jnp.where(lane < 16, middle, low)).astype(BF16)
    for k in range(16):
        out_ref[k, 128:144] = packed


def kernel_unpack(r_ref, e_ref, c_ref):
    rows = jnp.concatenate([r_ref[s, 128:144].astype(F32)[:2] for s in range(16)], axis=0)
    total = (rows + roll(rows, -8, 1)) + roll(rows, -16, 1)
    tall = total.T
    c_ref[0] = tall[:4]
    c_ref[1] = tall[4:8]
    for s in range(16):
        for pp in range(2):
            both = r_ref[s, pp * 64 : (pp + 1) * 64]
            e_ref[2 * s + pp, 0] = both[:, :64]
            e_ref[2 * s + pp, 1] = both[:, 64:]


def shape(dims, dtype):
    return jax.ShapeDtypeStruct(dims, dtype)


def run(kernel, outs, args, scratch=(), scalar=False, raw=False):
    in_specs = None
    if raw:
        in_specs = [pl.BlockSpec(memory_space=pltpu.SMEM)] + [pl.BlockSpec(memory_space=pltpu.HBM)] * (len(args) - 1)
    elif scalar:
        in_specs = [pl.BlockSpec(memory_space=pltpu.SMEM)] + [pl.BlockSpec(memory_space=pltpu.VMEM)] * (len(args) - 1)
    else:
        in_specs = [pl.BlockSpec(memory_space=pltpu.VMEM)] * len(args)
    return pl.pallas_call(
        kernel,
        out_shape=outs,
        in_specs=in_specs,
        out_specs=jax.tree.map(lambda _: pl.BlockSpec(memory_space=pltpu.VMEM), outs),
        scratch_shapes=list(scratch),
        compiler_params=pltpu.CompilerParams(vmem_limit_bytes=48 << 20),
    )(*args)


def phases(momenta, z_index):
    site = jnp.arange(4 * SITES, dtype=jnp.int32)
    turn_x = momenta[:, 0, None] * (site % LX)[None] % LX
    turn_y = momenta[:, 1, None] * (site // LX)[None] % LX
    turn_z = momenta[:, 2, None] * z_index % NZ
    angles = (
        2.0
        * math.pi
        * (turn_x.astype(F32) / LX + turn_y.astype(F32) / LX + turn_z.astype(F32) / NZ)
    )
    return jnp.concatenate([jnp.cos(angles), -jnp.sin(angles)], axis=0)


def swap(value, axes):
    return lax.all_to_all(value, axes, split_axis=0, concat_axis=0, tiled=True)


def spread(value, axes, count):
    return swap(jnp.broadcast_to(value[None], (count,) + value.shape), axes)


def local(eigvecs, gauge_links, perambulators, momenta):
    planes = ("zh", "zu", "zd", "yu", "yd")
    pairs_a = [(i, i ^ 1) for i in range(NZ)]
    pairs_b = [(i, ((i + 1) ^ 1) - 1) for i in range(NZ)]
    pairs_b = [(i, j % NZ) for i, j in pairs_b]
    ring_a = [(i, i ^ 1) for i in range(4)]
    ring_b = [(i, (((i + 1) ^ 1) - 1) % 4) for i in range(4)]
    z_index = lax.axis_index(planes)
    x_index = lax.axis_index("x")
    tm_index = lax.axis_index(("yh", "c"))
    odd = jnp.stack([lax.axis_index("yd"), x_index % 2]).astype(jnp.int32)

    field = eigvecs.reshape(6 * NEV, 1, SITES)
    links = gauge_links.reshape(54, 1, SITES)
    site_shape = shape((3, SITES, 128), F32)
    row_shape = shape((3, ROW, 128), F32)
    values, send_za, send_zb, send_xa, send_xb, cols = run(
        kernel_prepare,
        (site_shape, site_shape, site_shape, row_shape, row_shape, shape((SITES, 54), F32)),
        (
            odd,
            pltpu.with_memory_space_constraint(field, pltpu.HBM),
            pltpu.with_memory_space_constraint(links, pltpu.HBM),
        ),
        scratch=[
            pltpu.VMEM((6 * NEV, 1, SITES), F32),
            pltpu.VMEM((54, 1, SITES), F32),
            pltpu.SemaphoreType.DMA((2,)),
        ],
        raw=True,
    )
    recv_za = lax.ppermute(send_za, planes, pairs_a)
    recv_zb = lax.ppermute(send_zb, planes, pairs_b)
    recv_xa = lax.ppermute(send_xa, "x", ring_a)
    recv_xb = lax.ppermute(send_xb, "x", ring_b)

    inner = run(kernel_inner, site_shape, (values, cols))
    send = run(
        kernel_smear,
        shape((4, 3, SITES, 128), BF16),
        (odd, inner, cols, recv_za, recv_zb, recv_xa, recv_xb),
        scalar=True,
    )
    mine = lax.dynamic_index_in_dim(momenta.reshape(4, 4, 2, 3), x_index, 1, keepdims=False).reshape(8, 3)
    phase = phases(mine, z_index)
    send, phase = lax.optimization_barrier((send, phase))
    shared = swap(send, "x")
    scale = 1.0 / math.sqrt(3.0 * NZ * LX * LX)

    def contract(*refs):
        kernel_contract(*refs, scale=scale)

    partial = run(
        contract,
        shape((4, 4, 32, 128), F32),
        (shared, phase),
        scratch=[
            pltpu.VMEM((12 * SITES, 128), F32),
            pltpu.VMEM((12 * SITES, 128), F32),
            pltpu.VMEM((128, 12 * SITES), BF16),
            pltpu.VMEM((4, 12 * SITES, 256), BF16),
            pltpu.VMEM((8, 4 * SITES, 256), F32),
        ],
    )
    pieces = swap(partial.reshape(16, 32, 128), ("zu", "zd", "yu", "yd"))
    part = jnp.sum(pieces, axis=0)
    part, perambulators, send = lax.optimization_barrier((part, perambulators, send))
    prev = lax.ppermute(part, "zh", [(0, 1), (1, 2), (2, 0)])
    following = lax.ppermute(part, "zh", [(1, 0), (2, 1), (0, 2)])
    third = lax.axis_index("zh")
    term0 = jnp.where(third == 0, part, jnp.where(third == 1, prev, following))
    term1 = jnp.where(third == 1, part, jnp.where(third == 2, prev, following))
    term2 = jnp.where(third == 2, part, jnp.where(third == 0, prev, following))
    part = ((term0 + term1) + term2).astype(BF16)
    near = spread(part, ("zu", "yu", "yh", "c"), 16).reshape(4, 4, 32, 128)
    factors = run(kernel_factors, shape((4, 128, 16 * 128), BF16), (perambulators.reshape(4, 2, 16, NEV, NEV),))

    smeared = run(kernel_output, shape((2, 3, NEV, SITES), BF16), (send,))
    payload = run(
        kernel_correlate,
        shape((16, 144, 128), BF16),
        (tm_index.astype(jnp.int32).reshape(1), near, factors),
        scalar=True,
    )
    payload, smeared = lax.optimization_barrier((payload, smeared))
    everything = swap(payload, ("zd", "yd", "x"))
    elementals, correlator = run(kernel_unpack, (shape((32, 2, NEV, NEV), BF16), shape((2, 4, 32), F32)), (everything,))
    return (
        smeared.reshape(1, 2, 3, NEV, 1, SITES),
        elementals.reshape(32, 1, 2, NEV, NEV),
        jnp.swapaxes(correlator, 1, 2).reshape(2, 32, 1, 4),
    )


def solution(mesh):
    fine = Mesh(mesh.devices.reshape(3, 2, 2, 2, 2, 4, 2, 2), ("zh", "zu", "zd", "yu", "yd", "x", "yh", "c"))
    space = ("zh", "zu", "zd", "yu", "yd", "x")
    times = ("yh", "c")

    return jax.shard_map(
        local,
        mesh=fine,
        in_specs=(
            P(times, None, None, None, space, None),
            P(None, times, None, None, None, space, None),
            P(times, None, None, None, None, None, None),
            P(),
        ),
        out_specs=(
            P(times, None, None, None, space, None),
            P(None, times, None, None, None),
            P(None, None, times, None),
        ),
        check_vma=False,
    )
```
